256 devices in a mesh: lon: 16 (over x_hi, y, core), rad: 16 (over z, x_lo).
Axes of the slice: x: 4 (x_hi: 2, x_lo: 2; x = x_hi * 2 + x_lo), y: 4, z: 8, core: 2. Of those that a mesh axis runs over, the one named last changes fastest.
Arguments:
- state: float32 [5, 128, 48, 2048], P(None, 'rad', None, 'lon'), may hold values from -6 to 6
- outer_rows: float32 [5, 128, 4, 2048], P(None, 'rad', None, 'lon'), may hold values from -6 to 6
- kappa: float32 [128], P('rad'), may hold values from 5e-05 to 0.0005
Outputs:
- increment: float32 [5, 128, 48, 2048], P(None, 'rad', None, 'lon')
The draws below stay inside these ranges and needn't reach their ends.
All inputs are finite; a program needn't handle non-finite values.
Results may differ from the reference program's by a relative error of at most 0.00002.
Values sent between devices are 32-bit elements; how exact they have to be, the bound alone decides.
A program may use at most 128 MiB of HBM per device.

```python
import math
import jax
import jax.numpy as jnp
from jax import lax

LEV_DEV = 8
ROWS = 48
NLON = 2048
NLEV = 128
N_RAD = 16


def level_of(stream_key, shape, pieces, least, high):
    def one(axis_at, blocks):
        heights = jax.random.uniform(jax.random.fold_in(jax.random.fold_in(stream_key, 6), axis_at), (blocks,), jnp.float32, least / len(pieces), high / len(pieces))
        return jnp.repeat(jnp.exp(heights), shape[axis_at] // blocks).reshape((-1,) + (1,) * (len(shape) - axis_at - 1))

    gain = one(*pieces[0])
    for cut in pieces[1:]:
        gain = gain * one(*cut)
    return gain


def scatter_about(stream_key, extent, scale, bound, shards=(), kind=jnp.bfloat16):
    values = jax.random.normal(stream_key, extent, jnp.float32) * scale
    if len(shards) > 0:
        values = level_of(stream_key, extent, shards, -0.22, 0.18) * values
    return jnp.clip(values, min=-bound, max=bound).astype(kind)


def setup_inputs(seed: int = 0) -> dict:
    keys = jax.random.split(jax.random.key(seed), 4)
    return {
        "state": scatter_about(keys[0], (5, NLEV, ROWS, NLON), 1.0, 6.0, ((1, 16), (3, 16)), jnp.float32),
        "outer_rows": scatter_about(keys[1], (5, NLEV, 4, NLON), 1.0, 6.0, ((1, 16), (3, 16)), jnp.float32),
        "kappa": jnp.clip(jnp.exp(math.log(0.0005) - 2.3025852 * jax.random.uniform(keys[2], (NLEV,), jnp.float32) ** level_of(keys[2], (NLEV,), ((0, 16),), -0.2, 0.2)), 4.999999873689376e-05, 0.0005),
    }


first_coeffs = (0.8, -0.2, 4.0 / 105.0, -1.0 / 280.0)
second_coeffs = (-205.0 / 72.0, 1.6, -0.2, 8.0 / 315.0, -1.0 / 560.0)
time_step = 0.002
gamma_less_one = 0.4
radial_ratio = 3.0


def window(padded, offset, length, axis):
    return lax.slice_in_dim(padded, offset, offset + length, axis=axis)


def first_derivative(padded, length, axis):
    total = first_coeffs[0] * (window(padded, 5, length, axis) - window(padded, 3, length, axis))
    for reach in range(2, 5):
        total = total + first_coeffs[reach - 1] * (window(padded, 4 + reach, length, axis) - window(padded, 4 - reach, length, axis))
    return total


def second_derivative(padded, length, axis):
    total = second_coeffs[0] * window(padded, 4, length, axis)
    for reach in range(1, 5):
        total = total + second_coeffs[reach] * (window(padded, 4 + reach, length, axis) + window(padded, 4 - reach, length, axis))
    return total


def geometry(rows, nlon):
    index = jnp.arange(rows, dtype=jnp.float32)
    spacing = 2.0 * math.pi / nlon
    theta = (index + 0.5) * spacing
    metric = 1.0 / jnp.sin(theta)
    return metric[:, None], (jnp.cos(theta) * metric)[:, None]


def tendency(center, pad_lon, pad_row, pad_level, kappa_col, metric, curvature):
    levels, rows, width = center.shape[1], center.shape[2], center.shape[3]
    slope_lon = metric * first_derivative(pad_lon, width, 3)
    slope_row = first_derivative(pad_row, rows, 2)
    slope_level = radial_ratio * first_derivative(pad_level, levels, 1)
    wind_lon = center[1]
    wind_row = center[2]
    wind_level = center[3]
    temper = center[4]
    carried = wind_lon * slope_lon + wind_row * slope_row + wind_level * slope_level
    spread = slope_lon[1] + slope_row[2] + slope_level[3] + curvature * wind_row
    laplace = metric * metric * second_derivative(pad_lon[4], width, 2) + second_derivative(pad_row[4], rows, 1) + (radial_ratio * radial_ratio) * second_derivative(pad_level[4], levels, 0)
    return jnp.stack([
        -carried[0] - spread,
        -carried[1] - temper * slope_lon[0] - slope_lon[4],
        -carried[2] - temper * slope_row[0] - slope_row[4],
        -carried[3] - temper * slope_level[0] - slope_level[4],
        -carried[4] - gamma_less_one * temper * spread + kappa_col * laplace,
    ])


def section_tendency(fields, outer_rows, kappa, metric, curvature):
    flip_signs = jnp.array([1.0, -1.0, -1.0, 1.0, 1.0], dtype=jnp.float32).reshape(5, 1, 1, 1)
    pad_lon = jnp.concatenate([fields[..., -4:], fields, fields[..., :4]], axis=3)
    partner = jnp.roll(fields[:, :, :4, :], NLON // 2, axis=3)
    pad_row = jnp.concatenate([partner[:, :, ::-1, :] * flip_signs, fields, outer_rows], axis=2)
    pad_level = jnp.pad(fields, ((0, 0), (4, 4), (0, 0), (0, 0)))

    def block(start):
        center = lax.dynamic_slice_in_dim(fields, start, LEV_DEV, 1)
        piece_lon = lax.dynamic_slice_in_dim(pad_lon, start, LEV_DEV, 1)
        piece_row = lax.dynamic_slice_in_dim(pad_row, start, LEV_DEV, 1)
        piece_level = lax.dynamic_slice_in_dim(pad_level, start, LEV_DEV + 8, 1)
        kappa_col = lax.dynamic_slice_in_dim(kappa, start, LEV_DEV, 0).reshape(LEV_DEV, 1, 1)
        return tendency(center, piece_lon, piece_row, piece_level, kappa_col, metric, curvature)

    starts = jnp.arange(N_RAD, dtype=jnp.int32) * LEV_DEV
    blocks = lax.map(block, starts)
    return jnp.moveaxis(blocks, 0, 1).reshape(fields.shape)


def reference(state, outer_rows, kappa):
    metric, curvature = geometry(ROWS, NLON)
    first = section_tendency(state, outer_rows, kappa, metric, curvature)
    section = state + time_step * first
    second = section_tendency(section, outer_rows, kappa, metric, curvature)
    return 0.5 * time_step * (first + second)
```

```python
import functools
import math

import jax
import jax.numpy as jnp
from jax import lax
from jax.experimental import pallas as pl
from jax.experimental.pallas import tpu as pltpu
from jax.sharding import PartitionSpec as P

first_coeffs = (0.8, -0.2, 4.0 / 105.0, -1.0 / 280.0)
second_coeffs = (-205.0 / 72.0, 1.6, -0.2, 8.0 / 315.0, -1.0 / 560.0)
time_step = 0.002
gamma_less_one = 0.4
radial_ratio = 3.0

FIELDS, LEVELS, ROWS, WIDTH = 5, 8, 48, 128
CHUNK = 8
CHUNKS = ROWS // CHUNK
LAG = 2
MESH = pl.DeviceIdType.MESH
flip = (1.0, -1.0, -1.0, 1.0, 1.0)


def placed_at(lon, rad):
    return (lon // 2) * 2 + rad % 2, (rad // 2) * 2 + lon % 2


def by_row(values, sub):
    tile = jnp.full((CHUNK, WIDTH), values[0], jnp.float32)
    for r in range(1, CHUNK):
        tile = jnp.where(sub == r, jnp.float32(values[r]), tile)
    return tile


def kernel(
    lons, rads, state, outer, kappa, out,
    home, a, b, first, total, edge_out, edge_in, pole_out, pole_in, rows_in, kap_out, kap_in,
    home_sem, in_recv, in_send, lev_recv, lev_send, edge1_recv, edge1_send, edge2_recv, edge2_send,
    pole_recv, pole_send, rows_recv, rows_send, kap_recv, kap_send, out_recv, out_send,
):
    lon, rad = lax.axis_index("lon"), lax.axis_index("rad")
    at_lon, at_rad = placed_at(lon, rad)
    swapped = at_lon != lon
    stays = at_lon == lon
    below, above = at_rad > 0, at_rad < rads - 1
    half = lons // 2

    def around(g, by):
        return lax.rem(g + by + lons, lons)

    partner = (at_lon, at_rad)
    home_right = placed_at(around(lon, 1), rad)
    home_left = placed_at(around(lon, -1), rad)
    home_across = placed_at(around(lon, half), rad)
    right = placed_at(around(at_lon, 1), at_rad)
    left = placed_at(around(at_lon, -1), at_rad)
    across = placed_at(around(at_lon, half), at_rad)
    lower = placed_at(at_lon, jnp.maximum(at_rad - 1, 0))
    upper = placed_at(at_lon, jnp.minimum(at_rad + 1, rads - 1))
    from_right = (around(at_lon, 1), at_rad)
    from_left = (around(at_lon, -1), at_rad)
    from_across = (around(at_lon, half), at_rad)

    def remote(src, dst, send, recv, to):
        return pltpu.make_async_remote_copy(
            src_ref=src, dst_ref=dst, send_sem=send, recv_sem=recv, device_id=to, device_id_type=MESH
        )

    def rows_of(i):
        return pl.ds(CHUNK * i, CHUNK)

    def ext_rows(i):
        return pl.ds(8 + CHUNK * i, CHUNK)

    own = pl.ds(4, LEVELS)

    load_home = pltpu.make_async_copy(state, home, home_sem)
    load_home.start()
    keep = [
        pltpu.make_async_copy(state.at[:, :, rows_of(i), :], a.at[:, own, ext_rows(i), :], in_recv.at[i])
        for i in range(CHUNKS)
    ]
    keep_rows = pltpu.make_async_copy(outer, rows_in, rows_recv)

    @pl.when(stays)
    def _():
        for c in keep:
            c.start()
        keep_rows.start()

    barrier = pltpu.get_barrier_semaphore()
    for peer in (home_right, home_left, home_across, right, left, across, from_right, from_left, from_across):
        pl.semaphore_signal(barrier, inc=1, device_id=peer, device_id_type=MESH)

    @pl.when(swapped)
    def _():
        pl.semaphore_signal(barrier, inc=1, device_id=partner, device_id_type=MESH)

    @pl.when(below)
    def _():
        pl.semaphore_signal(barrier, inc=1, device_id=lower, device_id_type=MESH)

    @pl.when(above)
    def _():
        pl.semaphore_signal(barrier, inc=1, device_id=upper, device_id_type=MESH)

    sub = lax.broadcasted_iota(jnp.int32, (CHUNK, WIDTH), 0)
    lane = lax.broadcasted_iota(jnp.int32, (CHUNK, WIDTH), 1)
    group = lane // 4

    def empty_levels(start):
        @pl.loop(0, 4)
        def _(l):
            for f in range(FIELDS):
                for i in range(CHUNKS):
                    a[f, start + l, ext_rows(i), :] = jnp.zeros((CHUNK, WIDTH), jnp.float32)
                    b[f, start + l, ext_rows(i), :] = jnp.zeros((CHUNK, WIDTH), jnp.float32)

    @pl.when(at_rad == 0)
    def _():
        empty_levels(0)

    @pl.when(at_rad == rads - 1)
    def _():
        empty_levels(4 + LEVELS)

    kap = jnp.full((LEVELS, WIDTH), kappa[0], jnp.float32)
    for l in range(1, LEVELS):
        kap = jnp.where(sub == l, kappa[l], kap)
    kap_out[...] = kap

    @pl.when(stays)
    def _():
        kap_in[...] = kap

    def pack(sec, i, l, tiles):
        at = lax.rem(l, 4)
        to_left = edge_out[sec, 0, i, l // 4]
        to_right = edge_out[sec, 1, i, l // 4]
        for f in range(FIELDS):
            j = 4 * f + at
            mine = group == j
            to_left = jnp.where(mine, pltpu.roll(tiles[f], 4 * j, 1), to_left)
            to_right = jnp.where(mine, pltpu.roll(tiles[f], 4 * j + 4, 1), to_right)
        edge_out[sec, 0, i, l // 4] = to_left
        edge_out[sec, 1, i, l // 4] = to_right

    def pole_rows(sec, src, level, row):
        @pl.loop(0, LEVELS)
        def _(l):
            for f in range(FIELDS):
                for k in range(4):
                    value = src[f, level + l, pl.ds(row + 3 - k, 1), :]
                    pole_out[sec, f, l, pl.ds(k, 1), :] = -value if flip[f] < 0 else value

    load_home.wait()
    edge_out[...] = jnp.zeros_like(edge_out)

    @pl.loop(0, LEVELS)
    def _(l):
        for i in range(CHUNKS):
            pack(0, i, l, [home[f, l, rows_of(i), :] for f in range(FIELDS)])

    pole_rows(0, home, 0, 0)

    pl.semaphore_wait(
        barrier, 9 + swapped.astype(jnp.int32) + below.astype(jnp.int32) + above.astype(jnp.int32)
    )

    move = [
        remote(state.at[:, :, rows_of(i), :], a.at[:, own, ext_rows(i), :], in_send.at[i], in_recv.at[i], partner)
        for i in range(CHUNKS)
    ]
    move_rows = remote(outer, rows_in, rows_send, rows_recv, partner)
    move_kap = remote(kap_out, kap_in, kap_send, kap_recv, partner)
    edges1 = [
        remote(edge_out.at[0, 0], edge_in.at[0, 1], edge1_send.at[0], edge1_recv.at[1], home_left),
        remote(edge_out.at[0, 1], edge_in.at[0, 0], edge1_send.at[1], edge1_recv.at[0], home_right),
    ]
    poles = [
        remote(pole_out.at[0], pole_in.at[0], pole_send.at[0], pole_recv.at[0], home_across),
        remote(pole_out.at[1], pole_in.at[1], pole_send.at[1], pole_recv.at[1], across),
    ]

    def halo(sec, i, src, down_level, ext):
        buffer = a if sec == 0 else b
        rows = ext_rows(i) if ext else rows_of(i)
        down = remote(
            src.at[:, pl.ds(down_level, 4), rows, :], buffer.at[:, pl.ds(4 + LEVELS, 4), ext_rows(i), :],
            lev_send.at[sec, 0, i], lev_recv.at[sec, 1, i], lower,
        )
        up = remote(
            src.at[:, pl.ds(down_level + 4, 4), rows, :], buffer.at[:, pl.ds(0, 4), ext_rows(i), :],
            lev_send.at[sec, 1, i], lev_recv.at[sec, 0, i], upper,
        )
        return down, up

    def send_levels(sec, i, src, level, ext):
        down, up = halo(sec, i, src, level, ext)

        @pl.when(below)
        def _():
            down.start()

        @pl.when(above)
        def _():
            up.start()

    def await_levels(sec, i):
        down, up = halo(sec, i, a if sec == 0 else b, 4, True)

        @pl.when(below)
        def _():
            up.wait_recv()

        @pl.when(above)
        def _():
            down.wait_recv()

    @pl.when(swapped)
    def _():
        move[0].start()
        move[1].start()

    for c in edges1:
        c.start()
    poles[0].start()

    @pl.when(swapped)
    def _():
        move_kap.start()
        for c in move[2:]:
            c.start()
        move_rows.start()

    @pl.when(stays)
    def _():
        for i in range(CHUNKS):
            send_levels(0, i, state, 0, False)

    spacing = 2.0 * math.pi / (WIDTH * lons)

    def slopes(src, sec, i, l, metric):
        at = lax.rem(l, 4)
        from_l = edge_in[sec, 0, i, l // 4]
        from_r = edge_in[sec, 1, i, l // 4]
        row = 8 + CHUNK * i
        cells, by_lon, by_rows, by_level = [], [], [], []
        second = None
        for f in range(FIELDS):
            j = 4 * f + at
            q = src[f, l + 4, ext_rows(i), :]
            beyond = jnp.where(
                lane < 64, pltpu.roll(from_r, WIDTH - 4 * j, 1), pltpu.roll(from_l, WIDTH - 4 - 4 * j, 1)
            )
            d_lon = d_row = d_lev = e_lon = e_row = e_lev = None
            for k in range(1, 5):
                c = first_coeffs[k - 1]
                ahead = pltpu.roll(jnp.where(lane >= k, q, beyond), WIDTH - k, 1)
                behind = pltpu.roll(jnp.where(lane < WIDTH - k, q, beyond), k, 1)
                south = src[f, l + 4, pl.ds(row + k, CHUNK), :]
                north = src[f, l + 4, pl.ds(row - k, CHUNK), :]
                over = src[f, l + 4 + k, ext_rows(i), :]
                under = src[f, l + 4 - k, ext_rows(i), :]
                terms = (c * (ahead - behind), c * (south - north), (radial_ratio * c) * (over - under))
                d_lon, d_row, d_lev = terms if k == 1 else (d_lon + terms[0], d_row + terms[1], d_lev + terms[2])
                if f == 4:
                    e = second_coeffs[k]
                    terms = (e * (ahead + behind), e * (south + north), e * (over + under))
                    e_lon, e_row, e_lev = (
                        terms if k == 1 else (e_lon + terms[0], e_row + terms[1], e_lev + terms[2])
                    )
            if f == 4:
                middle = second_coeffs[0] * q
                second = (e_lon + middle, e_row + middle, e_lev + middle)
            cells.append(q)
            by_lon.append(metric * d_lon)
            by_rows.append(d_row)
            by_level.append(d_lev)
        return cells, by_lon, by_rows, by_level, second

    def tendency(src, sec, i, l, metric, curvature):
        cells, by_lon, by_rows, by_level, second = slopes(src, sec, i, l, metric)
        _, u_lon, u_row, u_lev, temper = cells
        carried = [u_lon * by_lon[f] + u_row * by_rows[f] + u_lev * by_level[f] for f in range(FIELDS)]
        spread = by_lon[1] + by_rows[2] + by_level[3] + curvature * u_row
        laplace = metric * metric * second[0] + second[1] + (radial_ratio * radial_ratio) * second[2]
        kap_l = jnp.broadcast_to(kap_in[pl.ds(l, 1), :], (CHUNK, WIDTH))
        return cells, [
            -carried[0] - spread,
            -carried[1] - temper * by_lon[0] - by_lon[4],
            -carried[2] - temper * by_rows[0] - by_rows[4],
            -carried[3] - temper * by_level[0] - by_level[4],
            -carried[4] - gamma_less_one * temper * spread + kap_l * laplace,
        ]

    def geometry(i):
        thetas = [(CHUNK * i + r + 0.5) * spacing for r in range(CHUNK)]
        return by_row([1.0 / math.sin(t) for t in thetas], sub), by_row(
            [math.cos(t) / math.sin(t) for t in thetas], sub
        )

    def first_section(i):
        metric, curvature = geometry(i)

        @pl.loop(0, LEVELS)
        def _(l):
            cells, rate = tendency(a, 0, i, l, metric, curvature)
            new = []
            for f in range(FIELDS):
                first[f, l, rows_of(i), :] = rate[f]
                new.append(cells[f] + time_step * rate[f])
                b[f, l + 4, ext_rows(i), :] = new[f]
            pack(1, i, l, new)

    def second_section(i):
        metric, curvature = geometry(i)

        @pl.loop(0, LEVELS)
        def _(l):
            _, rate = tendency(b, 1, i, l, metric, curvature)
            for f in range(FIELDS):
                total[f, l, rows_of(i), :] = (0.5 * time_step) * (first[f, l, rows_of(i), :] + rate[f])

    def edges2(i):
        return (
            remote(edge_out.at[1, 0, i], edge_in.at[1, 1, i], edge2_send.at[0, i], edge2_recv.at[1, i], left),
            remote(edge_out.at[1, 1, i], edge_in.at[1, 0, i], edge2_send.at[1, i], edge2_recv.at[0, i], right),
        )

    def take_pole(sec, dst):
        poles[sec].wait_recv()

        @pl.loop(0, LEVELS)
        def _(l):
            for f in range(FIELDS):
                dst[f, l + 4, pl.ds(4, 4), :] = pole_in[sec, f, l]

    give = [
        remote(total.at[:, :, rows_of(i), :], out.at[:, :, rows_of(i), :], out_send.at[i], out_recv.at[i], partner)
        for i in range(CHUNKS)
    ]
    put = [
        pltpu.make_async_copy(total.at[:, :, rows_of(i), :], out.at[:, :, rows_of(i), :], out_send.at[i])
        for i in range(CHUNKS)
    ]

    for t in range(CHUNKS + 1 + LAG):
        if t < CHUNKS:

            @pl.when(swapped)
            def _():
                move[t].wait_recv()
                send_levels(0, t, a, 4, True)

            @pl.when(stays)
            def _():
                keep[t].wait()

        i = t - 1
        if i == 0:
            for c in edges1:
                c.wait_recv()
            take_pole(0, a)

            @pl.when(swapped)
            def _():
                move_kap.wait_recv()

        if i == CHUNKS - 1:

            @pl.when(swapped)
            def _():
                move_rows.wait_recv()

            @pl.when(stays)
            def _():
                keep_rows.wait()

            @pl.loop(0, LEVELS)
            def _(l):
                for f in range(FIELDS):
                    a[f, l + 4, pl.ds(8 + ROWS, 4), :] = rows_in[f, l]
                    b[f, l + 4, pl.ds(8 + ROWS, 4), :] = rows_in[f, l]

        if 0 <= i < CHUNKS:
            await_levels(0, i)
            first_section(i)
            if i == 0:
                pole_rows(1, b, 4, 8)
                poles[1].start()
            send_levels(1, i, b, 4, True)
            for c in edges2(i):
                c.start()
        i = t - 1 - LAG
        if 0 <= i < CHUNKS:
            if i == 0:
                take_pole(1, b)
            await_levels(1, i)
            for c in edges2(i):
                c.wait_recv()
            second_section(i)

            @pl.when(swapped)
            def _():
                give[i].start()

            @pl.when(stays)
            def _():
                put[i].start()

    for c in (*edges1, *poles):
        c.wait_send()
    for i in range(CHUNKS):
        for c in edges2(i):
            c.wait_send()
        for sec in range(2):
            down, up = halo(sec, i, a if sec == 0 else b, 4, True)

            @pl.when(below)
            def _():
                down.wait_send()

            @pl.when(above)
            def _():
                up.wait_send()

    @pl.when(stays)
    def _():
        for c in put:
            c.wait()

    @pl.when(swapped)
    def _():
        for c in (*move, move_rows, move_kap):
            c.wait_send()
        for c in give:
            c.wait()


def solution(mesh):
    lons, rads = mesh.shape["lon"], mesh.shape["rad"]

    def on_device(state, outer_rows, kappa):
        f32 = jnp.float32
        vmem, dma = pltpu.VMEM, pltpu.SemaphoreType.DMA
        block = (FIELDS, LEVELS, ROWS, WIDTH)
        wide = (FIELDS, LEVELS + 8, ROWS + 16, WIDTH)
        edges = (2, 2, CHUNKS, 2, CHUNK, WIDTH)
        pole = (2, FIELDS, LEVELS, 4, WIDTH)
        return pl.pallas_call(
            functools.partial(kernel, lons, rads),
            out_shape=jax.ShapeDtypeStruct(block, f32),
            in_specs=[
                pl.BlockSpec(memory_space=pl.ANY),
                pl.BlockSpec(memory_space=pl.ANY),
                pl.BlockSpec(memory_space=pltpu.SMEM),
            ],
            out_specs=pl.BlockSpec(memory_space=pl.ANY),
            scratch_shapes=[
                vmem(block, f32), vmem(wide, f32), vmem(wide, f32), vmem(block, f32), vmem(block, f32),
                vmem(edges, f32), vmem(edges, f32), vmem(pole, f32), vmem(pole, f32),
                vmem((FIELDS, LEVELS, 4, WIDTH), f32), vmem((LEVELS, WIDTH), f32), vmem((LEVELS, WIDTH), f32),
                dma, dma((CHUNKS,)), dma((CHUNKS,)), dma((2, 2, CHUNKS)), dma((2, 2, CHUNKS)),
                dma((2,)), dma((2,)), dma((2, CHUNKS)), dma((2, CHUNKS)),
                dma((2,)), dma((2,)), dma, dma, dma, dma, dma((CHUNKS,)), dma((CHUNKS,)),
            ],
            compiler_params=pltpu.CompilerParams(
                collective_id=0, has_side_effects=True, vmem_limit_bytes=48 * 1024 * 1024
            ),
        )(state, outer_rows, kappa)

    placed = (P(None, "rad", None, "lon"), P(None, "rad", None, "lon"), P("rad"))
    return jax.shard_map(
        on_device, mesh=mesh, in_specs=placed, out_specs=P(None, "rad", None, "lon"), check_vma=False
    )
```

```python
import functools
import math

import jax
import jax.numpy as jnp
from jax import lax
from jax.experimental import pallas as pl
from jax.experimental.pallas import tpu as pltpu
from jax.sharding import PartitionSpec as P

first_coeffs = (0.8, -0.2, 4.0 / 105.0, -1.0 / 280.0)
second_coeffs = (-205.0 / 72.0, 1.6, -0.2, 8.0 / 315.0, -1.0 / 560.0)
time_step = 0.002
gamma_less_one = 0.4
radial_ratio = 3.0

FIELDS, LEVELS, ROWS, WIDTH = 5, 8, 48, 128
CHUNK = 8
CHUNKS = ROWS // CHUNK
LAG = 3
AHEAD = 4
UNROLL, UNROLL_LON = 2, 4
MESH = pl.DeviceIdType.MESH
flip = (1.0, -1.0, -1.0, 1.0, 1.0)


def placed_at(lon, rad, lons):
    odd = ((lon // 2) % (lons // 4) + lon // (lons // 2)) % 2
    return (lon // 2) * 2 + (rad + odd) % 2, (rad // 2) * 2 + (lon + odd) % 2


def by_row(values, sub):
    tile = jnp.full((CHUNK, WIDTH), values[0], jnp.float32)
    for r in range(1, CHUNK):
        tile = jnp.where(sub == r, jnp.float32(values[r]), tile)
    return tile


def kernel(
    lons, rads, state, outer, kappa, out,
    a, b, first, total, along, edge_own, edge_out, edge_in, pole_out, pole_in, rows_in, kap_out, kap_in, kap_s,
    kap_sem, in_recv, in_send, lev_recv, lev_send, edge_recv, edge_send,
    pole_recv, pole_send, rows_recv, rows_send, kap_recv, kap_send, out_recv, out_send,
):
    lon, rad = lax.axis_index("lon"), lax.axis_index("rad")
    at_lon, at_rad = placed_at(lon, rad, lons)
    swapped = at_lon != lon
    stays = at_lon == lon
    below, above = at_rad > 0, at_rad < rads - 1
    half = lons // 2

    def around(g, by):
        return lax.rem(g + by + lons, lons)

    partner = (at_lon, at_rad)
    right = placed_at(around(at_lon, 1), at_rad, lons)
    left = placed_at(around(at_lon, -1), at_rad, lons)
    across = placed_at(around(at_lon, half), at_rad, lons)
    lower = placed_at(at_lon, jnp.maximum(at_rad - 1, 0), lons)
    upper = placed_at(at_lon, jnp.minimum(at_rad + 1, rads - 1), lons)
    def remote(src, dst, send, recv, to):
        return pltpu.make_async_remote_copy(
            src_ref=src, dst_ref=dst, send_sem=send, recv_sem=recv, device_id=to, device_id_type=MESH
        )

    def rows_of(i):
        return pl.ds(CHUNK * i, CHUNK)

    def ext_rows(i):
        return pl.ds(8 + CHUNK * i, CHUNK)

    own = pl.ds(4, LEVELS)

    load_kap = pltpu.make_async_copy(kappa, kap_s, kap_sem)
    keep = [
        pltpu.make_async_copy(state.at[:, :, rows_of(i), :], a.at[:, own, ext_rows(i), :], in_recv.at[i])
        for i in range(CHUNKS)
    ]
    keep_rows = pltpu.make_async_copy(outer, rows_in, rows_recv)

    barrier = pltpu.get_barrier_semaphore()
    for peer in (right, left, across):
        pl.semaphore_signal(barrier, inc=1, device_id=peer, device_id_type=MESH)

    @pl.when(swapped)
    def _():
        pl.semaphore_signal(barrier, inc=1, device_id=partner, device_id_type=MESH)

    @pl.when(below)
    def _():
        pl.semaphore_signal(barrier, inc=1, device_id=lower, device_id_type=MESH)

    @pl.when(above)
    def _():
        pl.semaphore_signal(barrier, inc=1, device_id=upper, device_id_type=MESH)

    load_kap.start()

    @pl.when(stays)
    def _():
        for c in keep:
            c.start()
        keep_rows.start()

    sub = lax.broadcasted_iota(jnp.int32, (CHUNK, WIDTH), 0)
    lane = lax.broadcasted_iota(jnp.int32, (CHUNK, WIDTH), 1)
    group = lane // 8
    low = lane % 8 < 4
    across_seam = (lane < 4) | (lane >= WIDTH - 4)

    def empty_levels(start):
        @pl.loop(0, 4)
        def _(l):
            for f in range(FIELDS):
                for i in range(CHUNKS):
                    a[f, start + l, ext_rows(i), :] = jnp.zeros((CHUNK, WIDTH), jnp.float32)
                    b[f, start + l, ext_rows(i), :] = jnp.zeros((CHUNK, WIDTH), jnp.float32)

    @pl.when(at_rad == 0)
    def _():
        empty_levels(0)

    @pl.when(at_rad == rads - 1)
    def _():
        empty_levels(4 + LEVELS)

    edge_own[...] = jnp.zeros_like(edge_own)
    load_kap.wait()
    kap = jnp.full((LEVELS, WIDTH), kap_s[0], jnp.float32)
    for l in range(1, LEVELS):
        kap = jnp.where(sub == l, kap_s[l], kap)
    kap = kap * (time_step * second_coeffs[1])
    kap_out[...] = kap

    @pl.when(stays)
    def _():
        kap_in[...] = kap

    def put_edges(held, l, tiles):
        held = list(held)
        for f in range(FIELDS):
            at = 8 * (f % 2) + l
            held[f // 2] = jnp.where(group == at, pltpu.roll(tiles[f], (8 * at + 4) % WIDTH, 1), held[f // 2])
        return held

    def packed(src, level, row):
        held = [jnp.zeros((CHUNK, WIDTH), jnp.float32)] * 3
        for l in range(LEVELS):
            held = put_edges(held, l, [src[f, level + l, pl.ds(row, CHUNK), :] for f in range(FIELDS)])
        return held

    def post_edges(sec, i, held):
        edge_out[sec, 0, i, 0] = jnp.where(low, pltpu.roll(held[1], WIDTH - 4, 1), held[0])
        edge_out[sec, 0, i, 1] = held[2]
        edge_out[sec, 1, i, 0] = jnp.where(low, held[0], pltpu.roll(held[1], 4, 1))
        edge_out[sec, 1, i, 1] = held[2]

    def pole_rows(sec, src, level, row):
        mirror = lax.rem(11 - sub, 8)

        @pl.loop(0, LEVELS)
        def _(l):
            for f in range(FIELDS):
                value = jnp.take_along_axis(src[f, level + l, pl.ds(row, CHUNK), :], mirror, axis=0)
                pole_out[sec, f, l] = (-value if flip[f] < 0 else value)[:4]

    pl.semaphore_wait(
        barrier, 3 + swapped.astype(jnp.int32) + below.astype(jnp.int32) + above.astype(jnp.int32)
    )

    move = [
        remote(state.at[:, :, rows_of(i), :], a.at[:, own, ext_rows(i), :], in_send.at[i], in_recv.at[i], partner)
        for i in range(CHUNKS)
    ]
    move_rows = remote(outer, rows_in, rows_send, rows_recv, partner)
    move_kap = remote(kap_out, kap_in, kap_send, kap_recv, partner)
    poles = [
        remote(pole_out.at[n], pole_in.at[n], pole_send.at[n], pole_recv.at[n], across) for n in range(2)
    ]

    def edges(sec, i):
        return (
            remote(edge_out.at[sec, 0, i], edge_in.at[sec, 1, i], edge_send.at[sec, 0, i], edge_recv.at[sec, 1, i], left),
            remote(edge_out.at[sec, 1, i], edge_in.at[sec, 0, i], edge_send.at[sec, 1, i], edge_recv.at[sec, 0, i], right),
        )

    def halo(sec, i, src, down_level, ext):
        buffer = a if sec == 0 else b
        rows = ext_rows(i) if ext else rows_of(i)
        down = remote(
            src.at[:, pl.ds(down_level, 4), rows, :], buffer.at[:, pl.ds(4 + LEVELS, 4), ext_rows(i), :],
            lev_send.at[sec, 0, i], lev_recv.at[sec, 1, i], lower,
        )
        up = remote(
            src.at[:, pl.ds(down_level + 4, 4), rows, :], buffer.at[:, pl.ds(0, 4), ext_rows(i), :],
            lev_send.at[sec, 1, i], lev_recv.at[sec, 0, i], upper,
        )
        return down, up

    def send_levels(sec, i, src, level, ext):
        down, up = halo(sec, i, src, level, ext)

        @pl.when(below)
        def _():
            down.start()

        @pl.when(above)
        def _():
            up.start()

    def await_levels(sec, i):
        down, up = halo(sec, i, a if sec == 0 else b, 4, True)

        @pl.when(below)
        def _():
            up.wait_recv()

        @pl.when(above)
        def _():
            down.wait_recv()

    def send_edges(sec, i, src):
        if sec == 0:
            held = packed(src, 4, 8 + CHUNK * i)
            for n in range(3):
                edge_own[0, i, n] = held[n]
        else:
            held = [edge_own[1, i, n] for n in range(3)]
        post_edges(sec, i, held)
        for c in edges(sec, i):
            c.start()
        if i == 0:
            pole_rows(sec, src, 4, 8)
            poles[sec].start()

    @pl.when(swapped)
    def _():
        move_kap.start()
        for c in move[:AHEAD]:
            c.start()

    @pl.when(stays)
    def _():
        for i in range(CHUNKS):
            send_levels(0, i, state, 0, False)
        for i in range(CHUNKS):
            keep[i].wait()
            send_edges(0, i, a)

    spacing = 2.0 * math.pi / (WIDTH * lons)

    first_ratio = [c / first_coeffs[0] for c in first_coeffs]
    second_ratio = [e / second_coeffs[1] for e in second_coeffs[1:]]
    step = time_step * first_coeffs[0]

    def weighed(terms, ratios):
        return terms[0] + ratios[1] * terms[1] + ratios[2] * terms[2] + ratios[3] * terms[3]

    def seam(sec, i, own):
        left = [edge_in[sec, 0, i, n] for n in range(2)]
        right = [edge_in[sec, 1, i, n] for n in range(2)]
        beyond = (
            jnp.where(low, left[0], right[0]),
            jnp.where(low, pltpu.roll(left[0], WIDTH - 4, 1), pltpu.roll(right[0], 4, 1)),
            jnp.where(low, left[1], right[1]),
        )
        found = []
        for n in range(3):
            lack = beyond[n] - own[n]
            on_right = jnp.where(low, 0.0, lack)
            on_left = jnp.where(low, lack, 0.0)
            ahead = [pltpu.roll(on_right, WIDTH - k, 1) for k in range(1, 5)]
            behind = [pltpu.roll(on_left, k, 1) for k in range(1, 5)]
            d = jnp.where(low, weighed(ahead, first_ratio), -weighed(behind, first_ratio))
            if n == 2:
                e = jnp.where(low, weighed(ahead, second_ratio), weighed(behind, second_ratio))
                d = jnp.where(lane < 64, d, pltpu.roll(e, 64, 1))
            found.append(d)
        return found

    def turned(q, m, d, ratios, sign):
        even = ratios[2] * q + (0.5 * (ratios[1] + ratios[3])) * m
        odd = (0.5 * (ratios[3] - ratios[1])) * d
        ahead, behind = pltpu.roll(even + odd, WIDTH - 3, 1), pltpu.roll(even - odd, 3, 1)
        return d + (ahead - behind) if sign < 0 else m + (ahead + behind)

    def along_lon(src, i, extra):
        def seam_of(n, at):
            return jnp.where(across_seam, pltpu.roll(extra[n], WIDTH - 4 - 8 * at, 1), 0.0)

        @pl.loop(0, LEVELS, unroll=UNROLL_LON)
        def _(l):
            for f in range(FIELDS):
                q = src[f, l + 4, ext_rows(i), :]
                ahead, behind = pltpu.roll(q, WIDTH - 1, 1), pltpu.roll(q, 1, 1)
                m, d = ahead + behind, ahead - behind
                along[f, l] = turned(q, m, d, first_ratio, -1) + seam_of(f // 2, 8 * (f % 2) + l)
                if f == 4:
                    along[5, l] = turned(q, m, d, second_ratio, 1) + seam_of(2, 8 + l)

    def tendency(src, i, l, consts):
        stretch, turn, stretch2, centre = consts
        row = 8 + CHUNK * i
        cells = [src[f, l + 4, ext_rows(i), :] for f in range(FIELDS)]
        _, u_lon, u_row, u_lev, temper = cells
        by_lon = [along[f, l] for f in range(FIELDS)]
        by_rows, by_level = [], []
        for f in range(FIELDS):
            row_d, lev_d, row_s, lev_s = [], [], [], []
            for k in range(1, 5):
                south = src[f, l + 4, pl.ds(row + k, CHUNK), :]
                north = src[f, l + 4, pl.ds(row - k, CHUNK), :]
                over = src[f, l + 4 + k, ext_rows(i), :]
                under = src[f, l + 4 - k, ext_rows(i), :]
                row_d.append(south - north)
                lev_d.append(over - under)
                if f == 4:
                    row_s.append(south + north)
                    lev_s.append(over + under)
            by_rows.append(weighed(row_d, first_ratio))
            by_level.append(weighed(lev_d, first_ratio))
            if f == 4:
                laplace = (
                    stretch2 * along[5, l]
                    + weighed(row_s, second_ratio)
                    + (radial_ratio * radial_ratio) * weighed(lev_s, second_ratio)
                    + centre * temper
                )
        to_lon, to_row, to_lev = stretch * u_lon, step * u_row, (radial_ratio * step) * u_lev
        carried = [to_lon * by_lon[f] + to_row * by_rows[f] + to_lev * by_level[f] for f in range(FIELDS)]
        spread = stretch * by_lon[1] + step * (by_rows[2] + radial_ratio * by_level[3]) + turn * u_row
        kap_l = jnp.broadcast_to(kap_in[pl.ds(l, 1), :], (CHUNK, WIDTH))
        return cells, [
            carried[0] + spread,
            carried[1] + stretch * (temper * by_lon[0] + by_lon[4]),
            carried[2] + step * (temper * by_rows[0] + by_rows[4]),
            carried[3] + (radial_ratio * step) * (temper * by_level[0] + by_level[4]),
            carried[4] + (gamma_less_one * temper) * spread - kap_l * laplace,
        ]

    def geometry(i):
        thetas = [(CHUNK * i + r + 0.5) * spacing for r in range(CHUNK)]
        metric = [1.0 / math.sin(t) for t in thetas]
        return (
            by_row([step * m for m in metric], sub),
            by_row([time_step * math.cos(t) * m for t, m in zip(thetas, metric)], sub),
            by_row([m * m for m in metric], sub),
            by_row([second_coeffs[0] / second_coeffs[1] * (m * m + 1 + radial_ratio**2) for m in metric], sub),
        )

    def first_section(i):
        consts = geometry(i)
        along_lon(a, i, seam(0, i, [edge_own[0, i, n] for n in range(3)]))

        @pl.loop(0, LEVELS, unroll=UNROLL)
        def _(l):
            cells, rate = tendency(a, i, l, consts)
            new = []
            for f in range(FIELDS):
                first[f, l, rows_of(i), :] = rate[f]
                new.append(cells[f] - rate[f])
                b[f, l + 4, ext_rows(i), :] = new[f]
            held = put_edges([edge_own[1, i, n] for n in range(3)], l, new)
            for n in range(3):
                edge_own[1, i, n] = held[n]

    def second_section(i):
        consts = geometry(i)
        along_lon(b, i, seam(1, i, [edge_own[1, i, n] for n in range(3)]))

        @pl.loop(0, LEVELS, unroll=UNROLL)
        def _(l):
            _, rate = tendency(b, i, l, consts)
            for f in range(FIELDS):
                total[f, l, rows_of(i), :] = -0.5 * (first[f, l, rows_of(i), :] + rate[f])

    def take_pole(sec, dst):
        poles[sec].wait_recv()

        @pl.loop(0, LEVELS)
        def _(l):
            for f in range(FIELDS):
                dst[f, l + 4, pl.ds(4, 4), :] = pole_in[sec, f, l]

    give = [
        remote(total.at[:, :, rows_of(i), :], out.at[:, :, rows_of(i), :], out_send.at[i], out_recv.at[i], partner)
        for i in range(CHUNKS)
    ]
    put = [
        pltpu.make_async_copy(total.at[:, :, rows_of(i), :], out.at[:, :, rows_of(i), :], out_send.at[i])
        for i in range(CHUNKS)
    ]

    for t in range(CHUNKS + 1 + LAG):
        if t < CHUNKS:

            @pl.when(swapped)
            def _():
                move[t].wait_recv()
                send_levels(0, t, a, 4, True)
                send_edges(0, t, a)

        i = t - 1
        if i == 0:
            take_pole(0, a)

            @pl.when(swapped)
            def _():
                move_kap.wait_recv()

        if i == CHUNKS - 1:

            @pl.when(swapped)
            def _():
                move_rows.wait_recv()

            @pl.when(stays)
            def _():
                keep_rows.wait()

            @pl.loop(0, LEVELS)
            def _(l):
                for f in range(FIELDS):
                    a[f, l + 4, pl.ds(8 + ROWS, 4), :] = rows_in[f, l]
                    b[f, l + 4, pl.ds(8 + ROWS, 4), :] = rows_in[f, l]

        if 0 <= i < CHUNKS:
            await_levels(0, i)
            for c in edges(0, i):
                c.wait_recv()
            first_section(i)
            send_levels(1, i, b, 4, True)
            send_edges(1, i, b)
        if t + AHEAD < CHUNKS:

            @pl.when(swapped)
            def _():
                move[t + AHEAD].start()
                if t + AHEAD == CHUNKS - 1:
                    move_rows.start()
        i = t - 1 - LAG
        if 0 <= i < CHUNKS:
            if i == 0:
                take_pole(1, b)
            await_levels(1, i)
            for c in edges(1, i):
                c.wait_recv()
            second_section(i)

            @pl.when(swapped)
            def _():
                give[i].start()

            @pl.when(stays)
            def _():
                put[i].start()

    for c in poles:
        c.wait_send()
    for i in range(CHUNKS):
        for sec in range(2):
            for c in edges(sec, i):
                c.wait_send()
            down, up = halo(sec, i, a if sec == 0 else b, 4, True)

            @pl.when(below)
            def _():
                down.wait_send()

            @pl.when(above)
            def _():
                up.wait_send()

    @pl.when(stays)
    def _():
        for c in put:
            c.wait()

    @pl.when(swapped)
    def _():
        for c in (*move, move_rows, move_kap):
            c.wait_send()
        for c in give:
            c.wait()


def solution(mesh):
    lons, rads = mesh.shape["lon"], mesh.shape["rad"]

    def on_device(state, outer_rows, kappa):
        f32 = jnp.float32
        vmem, dma = pltpu.VMEM, pltpu.SemaphoreType.DMA
        block = (FIELDS, LEVELS, ROWS, WIDTH)
        wide = (FIELDS, LEVELS + 8, ROWS + 16, WIDTH)
        edges = (2, 2, CHUNKS, 2, CHUNK, WIDTH)
        own_edges = (2, CHUNKS, 3, CHUNK, WIDTH)
        pole = (2, FIELDS, LEVELS, 4, WIDTH)
        return pl.pallas_call(
            functools.partial(kernel, lons, rads),
            out_shape=jax.ShapeDtypeStruct(block, f32),
            in_specs=[
                pl.BlockSpec(memory_space=pltpu.HBM),
                pl.BlockSpec(memory_space=pltpu.HBM),
                pl.BlockSpec(memory_space=pltpu.HBM),
            ],
            out_specs=pl.BlockSpec(memory_space=pl.ANY),
            scratch_shapes=[
                vmem(wide, f32), vmem(wide, f32), vmem(block, f32), vmem(block, f32),
                vmem((FIELDS + 1, LEVELS, CHUNK, WIDTH), f32),
                vmem(own_edges, f32), vmem(edges, f32), vmem(edges, f32), vmem(pole, f32), vmem(pole, f32),
                vmem((FIELDS, LEVELS, 4, WIDTH), f32), vmem((LEVELS, WIDTH), f32), vmem((LEVELS, WIDTH), f32), pltpu.SMEM((LEVELS,), f32),
                dma, dma((CHUNKS,)), dma((CHUNKS,)), dma((2, 2, CHUNKS)), dma((2, 2, CHUNKS)),
                dma((2, 2, CHUNKS)), dma((2, 2, CHUNKS)),
                dma((2,)), dma((2,)), dma, dma, dma, dma, dma((CHUNKS,)), dma((CHUNKS,)),
            ],
            compiler_params=pltpu.CompilerParams(
                collective_id=0, has_side_effects=True, vmem_limit_bytes=66_000_000
            ),
        )(state, outer_rows, kappa)

    placed = (P(None, "rad", None, "lon"), P(None, "rad", None, "lon"), P("rad"))
    return jax.shard_map(
        on_device, mesh=mesh, in_specs=placed, out_specs=P(None, "rad", None, "lon"), check_vma=False
    )
```

```python
import functools
import math

import jax
import jax.numpy as jnp
from jax import lax
from jax.experimental import pallas as pl
from jax.experimental.pallas import tpu as pltpu
from jax.sharding import PartitionSpec as P

first_coeffs = (0.8, -0.2, 4.0 / 105.0, -1.0 / 280.0)
second_coeffs = (-205.0 / 72.0, 1.6, -0.2, 8.0 / 315.0, -1.0 / 560.0)
time_step = 0.002
gamma_less_one = 0.4
radial_ratio = 3.0
first_taps = (672.0, -168.0, 32.0, -3.0)
second_taps = (8064.0, -1008.0, 128.0, -9.0)

FIELDS, LEVELS, ROWS, WIDTH = 5, 8, 48, 128
CHUNK = 8
CHUNKS = ROWS // CHUNK
LAG, LAG_STAYS = 3, 5
AHEAD = 4
UNROLL = 2
MESH = pl.DeviceIdType.MESH
flip = (1.0, -1.0, -1.0, 1.0, 1.0)


def placed_at(lon, rad, lons):
    odd = ((lon // 2) % (lons // 4) + lon // (lons // 2)) % 2
    return (lon // 2) * 2 + (rad + odd) % 2, (rad // 2) * 2 + (lon + odd) % 2


def by_row(values, sub):
    tile = jnp.full((CHUNK, WIDTH), values[0], jnp.float32)
    for r in range(1, CHUNK):
        tile = jnp.where(sub == r, jnp.float32(values[r]), tile)
    return tile


def kernel(
    lons, rads, state, outer, kappa, out,
    home, home_out, a, b, first, total, along, edge_own, edge_out, edge_in, pole_out, pole_in, rows_in, kap_out, kap_in, taps, kap_s,
    home_sem, home_send, kap_sem, in_recv, in_send, lev_recv, lev_send, edge_recv, edge_send,
    pole_recv, pole_send, rows_recv, rows_send, kap_recv, kap_send, out_recv, out_send,
):
    lon, rad = lax.axis_index("lon"), lax.axis_index("rad")
    at_lon, at_rad = placed_at(lon, rad, lons)
    swapped = at_lon != lon
    stays = at_lon == lon
    below, above = at_rad > 0, at_rad < rads - 1
    half = lons // 2
    home_side, side_of_pair = lon % 2, at_lon % 2
    sibling = (lon + 1 - 2 * home_side, rad)

    def around(g, by):
        return lax.rem(g + by + lons, lons)

    partner = (at_lon, at_rad)
    right = placed_at(around(at_lon, 1), at_rad, lons)
    left = placed_at(around(at_lon, -1), at_rad, lons)
    across = placed_at(around(at_lon, half), at_rad, lons)
    lower = placed_at(at_lon, jnp.maximum(at_rad - 1, 0), lons)
    upper = placed_at(at_lon, jnp.minimum(at_rad + 1, rads - 1), lons)
    def remote(src, dst, send, recv, to):
        return pltpu.make_async_remote_copy(
            src_ref=src, dst_ref=dst, send_sem=send, recv_sem=recv, device_id=to, device_id_type=MESH
        )

    def rows_of(i):
        return pl.ds(CHUNK * i, CHUNK)

    def ext_rows(i):
        return pl.ds(8 + CHUNK * i, CHUNK)

    own = pl.ds(4, LEVELS)

    load_home = pltpu.make_async_copy(state, home, home_sem)
    load_kap = pltpu.make_async_copy(kappa, kap_s, kap_sem)
    keep = [
        pltpu.make_async_copy(state.at[:, :, rows_of(i), :], a.at[:, own, ext_rows(i), :], in_recv.at[i])
        for i in range(CHUNKS)
    ]
    keep_rows = pltpu.make_async_copy(outer, rows_in, rows_recv)

    barrier = pltpu.get_barrier_semaphore()
    for peer in (right, left, across):
        pl.semaphore_signal(barrier, inc=1, device_id=peer, device_id_type=MESH)

    @pl.when(swapped)
    def _():
        pl.semaphore_signal(barrier, inc=1, device_id=partner, device_id_type=MESH)

    @pl.when(below)
    def _():
        pl.semaphore_signal(barrier, inc=1, device_id=lower, device_id_type=MESH)

    @pl.when(above)
    def _():
        pl.semaphore_signal(barrier, inc=1, device_id=upper, device_id_type=MESH)

    load_kap.start()

    @pl.when(swapped)
    def _():
        load_home.start()

    @pl.when(stays)
    def _():
        for c in keep:
            c.start()
        keep_rows.start()

    sub = lax.broadcasted_iota(jnp.int32, (CHUNK, WIDTH), 0)
    lane = lax.broadcasted_iota(jnp.int32, (CHUNK, WIDTH), 1)
    group = lane // 8
    low = lane % 8 < 4
    across_seam = (lane < 4) | (lane >= WIDTH - 4)

    def empty_levels(start):
        @pl.loop(0, 4)
        def _(l):
            for f in range(FIELDS):
                for i in range(CHUNKS):
                    a[f, start + l, ext_rows(i), :] = jnp.zeros((CHUNK, WIDTH), jnp.float32)
                    b[f, start + l, ext_rows(i), :] = jnp.zeros((CHUNK, WIDTH), jnp.float32)

    @pl.when(at_rad == 0)
    def _():
        empty_levels(0)

    @pl.when(at_rad == rads - 1)
    def _():
        empty_levels(4 + LEVELS)

    def put_edges(held, l, tiles):
        held = list(held)
        for f in range(FIELDS):
            at = 8 * (f % 2) + l
            held[f // 2] = jnp.where(group == at, pltpu.roll(tiles[f], (8 * at + 4) % WIDTH, 1), held[f // 2])
        return held

    def packed(src, level, row):
        held = [jnp.zeros((CHUNK, WIDTH), jnp.float32)] * 3
        for l in range(LEVELS):
            held = put_edges(held, l, [src[f, level + l, pl.ds(row, CHUNK), :] for f in range(FIELDS)])
        return held

    def post_edges(posted, i, held):
        posted[0, i, 0] = jnp.where(low, pltpu.roll(held[1], WIDTH - 4, 1), held[0])
        posted[0, i, 1] = held[2]
        posted[1, i, 0] = jnp.where(low, held[0], pltpu.roll(held[1], 4, 1))
        posted[1, i, 1] = held[2]

    def pole_rows(sec, src, level, row):
        mirror = lax.rem(11 - sub, 8)

        @pl.loop(0, LEVELS)
        def _(l):
            for f in range(FIELDS):
                value = jnp.take_along_axis(src[f, level + l, pl.ds(row, CHUNK), :], mirror, axis=0)
                pole_out[sec, f, l] = (-value if flip[f] < 0 else value)[:4]

    load_kap.wait()
    kap = jnp.full((LEVELS, WIDTH), kap_s[0], jnp.float32)
    for l in range(1, LEVELS):
        kap = jnp.where(sub == l, kap_s[l], kap)
    kap = kap * (time_step * second_coeffs[1])
    kap_out[...] = kap

    @pl.when(stays)
    def _():
        kap_in[...] = kap

    pl.semaphore_wait(
        barrier, 3 + swapped.astype(jnp.int32) + below.astype(jnp.int32) + above.astype(jnp.int32)
    )

    move = [
        remote(state.at[:, :, rows_of(i), :], a.at[:, own, ext_rows(i), :], in_send.at[i], in_recv.at[i], partner)
        for i in range(CHUNKS)
    ]
    move_rows = remote(outer, rows_in, rows_send, rows_recv, partner)
    move_kap = remote(kap_out, kap_in, kap_send, kap_recv, partner)
    poles = [
        remote(pole_out.at[n], pole_in.at[n], pole_send.at[n], pole_recv.at[n], across) for n in range(2)
    ]

    def edges(sec, i):
        return (
            remote(edge_out.at[sec, 0, i], edge_in.at[sec, 1, i], edge_send.at[sec, 0, i], edge_recv.at[sec, 1, i], left),
            remote(edge_out.at[sec, 1, i], edge_in.at[sec, 0, i], edge_send.at[sec, 1, i], edge_recv.at[sec, 0, i], right),
        )

    def halo(sec, i, src, down_level, ext):
        buffer = a if sec == 0 else b
        rows = ext_rows(i) if ext else rows_of(i)
        down = remote(
            src.at[:, pl.ds(down_level, 4), rows, :], buffer.at[:, pl.ds(4 + LEVELS, 4), ext_rows(i), :],
            lev_send.at[sec, 0, i], lev_recv.at[sec, 1, i], lower,
        )
        up = remote(
            src.at[:, pl.ds(down_level + 4, 4), rows, :], buffer.at[:, pl.ds(0, 4), ext_rows(i), :],
            lev_send.at[sec, 1, i], lev_recv.at[sec, 0, i], upper,
        )
        return down, up

    def send_levels(sec, i, src, level, ext):
        down, up = halo(sec, i, src, level, ext)

        @pl.when(below)
        def _():
            down.start()

        @pl.when(above)
        def _():
            up.start()

    def await_levels(sec, i):
        down, up = halo(sec, i, a if sec == 0 else b, 4, True)

        @pl.when(below)
        def _():
            up.wait_recv()

        @pl.when(above)
        def _():
            down.wait_recv()

    def each_edge(sec, i, act):
        to_left, to_right = edges(sec, i)
        if sec == 1:
            act(to_left)
            act(to_right)
        else:

            @pl.when(stays | (side_of_pair == 0))
            def _():
                act(to_left)

            @pl.when(stays | (side_of_pair == 1))
            def _():
                act(to_right)

    home_edges = [
        remote(home_out.at[1 - home_side, i], edge_in.at[0, home_side, i], home_send.at[i],
               edge_recv.at[0, home_side, i], sibling)
        for i in range(CHUNKS)
    ]

    def send_edges(sec, i, src):
        if sec == 0:
            held = packed(src, 4, 8 + CHUNK * i)
        else:
            held = [edge_own[i, n] for n in range(3)]
        post_edges(edge_out.at[sec], i, held)
        each_edge(sec, i, lambda c: c.start())
        if i == 0:
            pole_rows(sec, src, 4, 8)
            poles[sec].start()

    @pl.when(swapped)
    def _():
        move_kap.start()
        for c in move[:AHEAD]:
            c.start()

    @pl.when(stays)
    def _():
        for i in range(CHUNKS):
            send_levels(0, i, state, 0, False)

    @pl.when(stays)
    def _():
        for i in range(CHUNKS):
            keep[i].wait()
            send_edges(0, i, a)

    @pl.when(swapped)
    def _():
        load_home.wait()

        @pl.loop(0, CHUNKS)
        def _(i):
            post_edges(home_out, i, packed(home, 0, pl.multiple_of(CHUNK * i, CHUNK)))

        for c in home_edges:
            c.start()

    edge_own[...] = jnp.zeros_like(edge_own)
    tap = lax.broadcasted_iota(jnp.int32, (WIDTH, WIDTH), 0) - lax.broadcasted_iota(jnp.int32, (WIDTH, WIDTH), 1)
    for n, (weights, sign) in enumerate(((first_taps, -1.0), (second_taps, 1.0))):
        matrix = jnp.zeros((WIDTH, WIDTH), jnp.float32)
        for k in range(1, 5):
            matrix = jnp.where(tap == k, weights[k - 1], jnp.where(tap == -k, sign * weights[k - 1], matrix))
        for part in range(3):
            taps[n, pl.ds(WIDTH * part, WIDTH), :] = matrix.astype(jnp.bfloat16)

    spacing = 2.0 * math.pi / (WIDTH * lons)

    first_ratio = [c / first_coeffs[0] for c in first_coeffs]
    second_ratio = [e / second_coeffs[1] for e in second_coeffs[1:]]
    step = time_step * first_coeffs[0]

    def weighed(terms, ratios):
        return terms[0] + ratios[1] * terms[1] + ratios[2] * terms[2] + ratios[3] * terms[3]

    def summed(terms, weights):
        return weights[0] * terms[0] + weights[1] * terms[1] + weights[2] * terms[2] + weights[3] * terms[3]

    def seam(sec, i):
        left = [edge_in[sec, 0, i, n] for n in range(2)]
        right = [edge_in[sec, 1, i, n] for n in range(2)]
        beyond = (
            jnp.where(low, left[0], right[0]),
            jnp.where(low, pltpu.roll(left[0], WIDTH - 4, 1), pltpu.roll(right[0], 4, 1)),
            jnp.where(low, left[1], right[1]),
        )
        found = []
        for n in range(3):
            lack = beyond[n]
            on_right = jnp.where(low, 0.0, lack)
            on_left = jnp.where(low, lack, 0.0)
            ahead = [pltpu.roll(on_right, WIDTH - k, 1) for k in range(1, 5)]
            behind = [pltpu.roll(on_left, k, 1) for k in range(1, 5)]
            d = jnp.where(low, summed(ahead, first_taps), -summed(behind, first_taps))
            if n == 2:
                e = jnp.where(low, summed(ahead, second_taps), summed(behind, second_taps))
                d = jnp.where(lane < 64, d, pltpu.roll(e, 64, 1))
            found.append(d)
        return found

    def along_lon(src, i):
        q = src[:, own, ext_rows(i), :].reshape(FIELDS * LEVELS * CHUNK, WIDTH)
        high = q.astype(jnp.bfloat16)
        rest = q - high.astype(jnp.float32)
        middle = rest.astype(jnp.bfloat16)
        last = (rest - middle.astype(jnp.float32)).astype(jnp.bfloat16)
        parts = jnp.concatenate([high, middle, last], axis=1)
        slope = jnp.dot(parts, taps[0], preferred_element_type=jnp.float32)
        along[:FIELDS] = slope.reshape(FIELDS, LEVELS, CHUNK, WIDTH)
        second = jnp.dot(parts[4 * LEVELS * CHUNK :], taps[1], preferred_element_type=jnp.float32)
        along[FIELDS] = second.reshape(LEVELS, CHUNK, WIDTH)

    def tendency(src, i, l, extra, consts):
        stretch, turn, stretch2, centre = consts
        row = 8 + CHUNK * i
        cells = [src[f, l + 4, ext_rows(i), :] for f in range(FIELDS)]
        _, u_lon, u_row, u_lev, temper = cells

        def seam_of(n, at):
            return jnp.where(across_seam, pltpu.roll(extra[n], WIDTH - 4 - 8 * at, 1), 0.0)

        by_lon = [along[f, l] + seam_of(f // 2, 8 * (f % 2) + l) for f in range(FIELDS)]
        by_rows, by_level = [], []
        for f in range(FIELDS):
            row_d, lev_d, row_s, lev_s = [], [], [], []
            for k in range(1, 5):
                south = src[f, l + 4, pl.ds(row + k, CHUNK), :]
                north = src[f, l + 4, pl.ds(row - k, CHUNK), :]
                over = src[f, l + 4 + k, ext_rows(i), :]
                under = src[f, l + 4 - k, ext_rows(i), :]
                row_d.append(south - north)
                lev_d.append(over - under)
                if f == 4:
                    row_s.append(south + north)
                    lev_s.append(over + under)
            by_rows.append(weighed(row_d, first_ratio))
            by_level.append(weighed(lev_d, first_ratio))
            if f == 4:
                laplace = (
                    stretch2 * (along[FIELDS, l] + seam_of(2, 8 + l))
                    + weighed(row_s, second_ratio)
                    + (radial_ratio * radial_ratio) * weighed(lev_s, second_ratio)
                    + centre * temper
                )
        to_lon, to_row, to_lev = stretch * u_lon, step * u_row, (radial_ratio * step) * u_lev
        carried = [to_lon * by_lon[f] + to_row * by_rows[f] + to_lev * by_level[f] for f in range(FIELDS)]
        spread = stretch * by_lon[1] + step * (by_rows[2] + radial_ratio * by_level[3]) + turn * u_row
        kap_l = jnp.broadcast_to(kap_in[pl.ds(l, 1), :], (CHUNK, WIDTH))
        return cells, [
            carried[0] + spread,
            carried[1] + stretch * (temper * by_lon[0] + by_lon[4]),
            carried[2] + step * (temper * by_rows[0] + by_rows[4]),
            carried[3] + (radial_ratio * step) * (temper * by_level[0] + by_level[4]),
            carried[4] + (gamma_less_one * temper) * spread - kap_l * laplace,
        ]

    def geometry(i):
        thetas = [(CHUNK * i + r + 0.5) * spacing for r in range(CHUNK)]
        metric = [1.0 / math.sin(t) for t in thetas]
        return (
            by_row([time_step / 840 * m for m in metric], sub),
            by_row([time_step * math.cos(t) * m for t, m in zip(thetas, metric)], sub),
            by_row([m * m / second_taps[0] for m in metric], sub),
            by_row([second_coeffs[0] / second_coeffs[1] * (m * m + 1 + radial_ratio**2) for m in metric], sub),
        )

    def first_section(i):
        consts = geometry(i)
        extra = seam(0, i)
        along_lon(a, i)

        @pl.loop(0, LEVELS, unroll=UNROLL)
        def _(l):
            cells, rate = tendency(a, i, l, extra, consts)
            new = []
            for f in range(FIELDS):
                first[f, l, rows_of(i), :] = rate[f]
                new.append(cells[f] - rate[f])
                b[f, l + 4, ext_rows(i), :] = new[f]
            held = put_edges([edge_own[i, n] for n in range(3)], l, new)
            for n in range(3):
                edge_own[i, n] = held[n]

    def second_section(i):
        consts = geometry(i)
        extra = seam(1, i)
        along_lon(b, i)

        @pl.loop(0, LEVELS, unroll=UNROLL)
        def _(l):
            _, rate = tendency(b, i, l, extra, consts)
            for f in range(FIELDS):
                total[f, l, rows_of(i), :] = -0.5 * (first[f, l, rows_of(i), :] + rate[f])

    def take_pole(sec, dst):
        poles[sec].wait_recv()

        @pl.loop(0, LEVELS)
        def _(l):
            for f in range(FIELDS):
                dst[f, l + 4, pl.ds(4, 4), :] = pole_in[sec, f, l]

    give = [
        remote(total.at[:, :, rows_of(i), :], out.at[:, :, rows_of(i), :], out_send.at[i], out_recv.at[i], partner)
        for i in range(CHUNKS)
    ]
    put = [
        pltpu.make_async_copy(total.at[:, :, rows_of(i), :], out.at[:, :, rows_of(i), :], out_send.at[i])
        for i in range(CHUNKS)
    ]

    def finish(i, copies):
        if i == 0:
            take_pole(1, b)
        await_levels(1, i)
        for c in edges(1, i):
            c.wait_recv()
        second_section(i)
        copies[i].start()

    for t in range(CHUNKS + 1 + max(LAG, LAG_STAYS)):
        if t < CHUNKS:

            @pl.when(swapped)
            def _():
                move[t].wait_recv()
                send_levels(0, t, a, 4, True)
                send_edges(0, t, a)

        i = t - 1
        if i == 0:
            take_pole(0, a)

            @pl.when(swapped)
            def _():
                move_kap.wait_recv()

        if i == CHUNKS - 1:

            @pl.when(swapped)
            def _():
                move_rows.wait_recv()

            @pl.when(stays)
            def _():
                keep_rows.wait()

            @pl.loop(0, LEVELS)
            def _(l):
                for f in range(FIELDS):
                    a[f, l + 4, pl.ds(8 + ROWS, 4), :] = rows_in[f, l]
                    b[f, l + 4, pl.ds(8 + ROWS, 4), :] = rows_in[f, l]

        if 0 <= i < CHUNKS:
            await_levels(0, i)
            for c in edges(0, i):
                c.wait_recv()
            first_section(i)
            send_levels(1, i, b, 4, True)
            send_edges(1, i, b)
        if t + AHEAD < CHUNKS:

            @pl.when(swapped)
            def _():
                move[t + AHEAD].start()
                if t + AHEAD == CHUNKS - 1:
                    move_rows.start()
        if 0 <= t - 1 - LAG < CHUNKS:

            @pl.when(swapped)
            def _():
                finish(t - 1 - LAG, give)

        if 0 <= t - 1 - LAG_STAYS < CHUNKS:

            @pl.when(stays)
            def _():
                finish(t - 1 - LAG_STAYS, put)

    for c in poles:
        c.wait_send()
    for i in range(CHUNKS):
        for sec in range(2):
            each_edge(sec, i, lambda c: c.wait_send())
            down, up = halo(sec, i, a if sec == 0 else b, 4, True)

            @pl.when(below)
            def _():
                down.wait_send()

            @pl.when(above)
            def _():
                up.wait_send()

    @pl.when(stays)
    def _():
        for c in put:
            c.wait()

    @pl.when(swapped)
    def _():
        for c in (*move, *home_edges, move_rows, move_kap):
            c.wait_send()
        for c in give:
            c.wait()


def solution(mesh):
    lons, rads = mesh.shape["lon"], mesh.shape["rad"]

    def on_device(state, outer_rows, kappa):
        f32 = jnp.float32
        vmem, dma = pltpu.VMEM, pltpu.SemaphoreType.DMA
        block = (FIELDS, LEVELS, ROWS, WIDTH)
        wide = (FIELDS, LEVELS + 8, ROWS + 16, WIDTH)
        edges = (2, 2, CHUNKS, 2, CHUNK, WIDTH)
        own_edges = (CHUNKS, 3, CHUNK, WIDTH)
        pole = (2, FIELDS, LEVELS, 4, WIDTH)
        return pl.pallas_call(
            functools.partial(kernel, lons, rads),
            out_shape=jax.ShapeDtypeStruct(block, f32),
            in_specs=[
                pl.BlockSpec(memory_space=pltpu.HBM),
                pl.BlockSpec(memory_space=pltpu.HBM),
                pl.BlockSpec(memory_space=pltpu.HBM),
            ],
            out_specs=pl.BlockSpec(memory_space=pl.ANY),
            scratch_shapes=[
                vmem(block, f32), vmem((2, CHUNKS, 2, CHUNK, WIDTH), f32),
                vmem(wide, f32), vmem(wide, f32), vmem(block, f32), vmem(block, f32),
                vmem((FIELDS + 1, LEVELS, CHUNK, WIDTH), f32),
                vmem(own_edges, f32), vmem(edges, f32), vmem(edges, f32), vmem(pole, f32), vmem(pole, f32),
                vmem((FIELDS, LEVELS, 4, WIDTH), f32), vmem((LEVELS, WIDTH), f32), vmem((LEVELS, WIDTH), f32),
                vmem((2, 3 * WIDTH, WIDTH), jnp.bfloat16), pltpu.SMEM((LEVELS,), f32),
                dma, dma((CHUNKS,)), dma, dma((CHUNKS,)), dma((CHUNKS,)), dma((2, 2, CHUNKS)), dma((2, 2, CHUNKS)),
                dma((2, 2, CHUNKS)), dma((2, 2, CHUNKS)),
                dma((2,)), dma((2,)), dma, dma, dma, dma, dma((CHUNKS,)), dma((CHUNKS,)),
            ],
            compiler_params=pltpu.CompilerParams(
                collective_id=0, has_side_effects=True, vmem_limit_bytes=48_000_000
            ),
        )(*(pltpu.with_memory_space_constraint(x, pltpu.HBM) for x in (state, outer_rows, kappa)))

    placed = (P(None, "rad", None, "lon"), P(None, "rad", None, "lon"), P("rad"))
    return jax.shard_map(
        on_device, mesh=mesh, in_specs=placed, out_specs=P(None, "rad", None, "lon"), check_vma=False
    )
```

```python
import functools
import math

import jax
import jax.numpy as jnp
from jax import lax
from jax.experimental import pallas as pl
from jax.experimental.pallas import tpu as pltpu
from jax.sharding import PartitionSpec as P

first_coeffs = (0.8, -0.2, 4.0 / 105.0, -1.0 / 280.0)
second_coeffs = (-205.0 / 72.0, 1.6, -0.2, 8.0 / 315.0, -1.0 / 560.0)
time_step = 0.002
gamma_less_one = 0.4
radial_ratio = 3.0
first_taps = (672.0, -168.0, 32.0, -3.0)
second_taps = (8064.0, -1008.0, 128.0, -9.0)

FIELDS, LEVELS, ROWS, WIDTH = 5, 8, 48, 128
CHUNK = 8
CHUNKS = ROWS // CHUNK
LAG, LAG_STAYS = 3, 5
AHEAD = 4
UNROLL = 4
MESH = pl.DeviceIdType.MESH
flip = (1.0, -1.0, -1.0, 1.0, 1.0)


def placed_at(lon, rad, lons):
    odd = ((lon // 2) % (lons // 4) + lon // (lons // 2)) % 2
    return (lon // 2) * 2 + (rad + odd) % 2, (rad // 2) * 2 + (lon + odd) % 2


def by_row(values, sub):
    tile = jnp.full((CHUNK, WIDTH), values[0], jnp.float32)
    for r in range(1, CHUNK):
        tile = jnp.where(sub == r, jnp.float32(values[r]), tile)
    return tile


def kernel(
    lons, rads, state, outer, kappa, out,
    home, home_out, a, b, first, total, along, south_d, up_d, rest, edge_own, edge_out, edge_in, pole_out, pole_in, rows_in, kap_out, kap_in, taps, kap_s,
    home_sem, home_send, kap_sem, in_recv, in_send, lev_recv, lev_send, edge_recv, edge_send,
    pole_recv, pole_send, rows_recv, rows_send, kap_recv, kap_send, out_recv, out_send,
):
    lon, rad = lax.axis_index("lon"), lax.axis_index("rad")
    at_lon, at_rad = placed_at(lon, rad, lons)
    swapped = at_lon != lon
    stays = at_lon == lon
    below, above = at_rad > 0, at_rad < rads - 1
    half = lons // 2
    home_side, side_of_pair = lon % 2, at_lon % 2
    sibling = (lon + 1 - 2 * home_side, rad)

    def around(g, by):
        return lax.rem(g + by + lons, lons)

    partner = (at_lon, at_rad)
    right = placed_at(around(at_lon, 1), at_rad, lons)
    left = placed_at(around(at_lon, -1), at_rad, lons)
    across = placed_at(around(at_lon, half), at_rad, lons)
    lower = placed_at(at_lon, jnp.maximum(at_rad - 1, 0), lons)
    upper = placed_at(at_lon, jnp.minimum(at_rad + 1, rads - 1), lons)
    def remote(src, dst, send, recv, to):
        return pltpu.make_async_remote_copy(
            src_ref=src, dst_ref=dst, send_sem=send, recv_sem=recv, device_id=to, device_id_type=MESH
        )

    def rows_of(i):
        return pl.ds(CHUNK * i, CHUNK)

    def ext_rows(i):
        return pl.ds(8 + CHUNK * i, CHUNK)

    own = pl.ds(4, LEVELS)

    load_home = pltpu.make_async_copy(state, home, home_sem)
    load_kap = pltpu.make_async_copy(kappa, kap_s, kap_sem)
    keep = [
        pltpu.make_async_copy(state.at[:, :, rows_of(i), :], a.at[:, own, ext_rows(i), :], in_recv.at[i])
        for i in range(CHUNKS)
    ]
    keep_rows = pltpu.make_async_copy(outer, rows_in, rows_recv)

    barrier = pltpu.get_barrier_semaphore()
    for peer in (right, left, across):
        pl.semaphore_signal(barrier, inc=1, device_id=peer, device_id_type=MESH)

    @pl.when(swapped)
    def _():
        pl.semaphore_signal(barrier, inc=1, device_id=partner, device_id_type=MESH)

    @pl.when(below)
    def _():
        pl.semaphore_signal(barrier, inc=1, device_id=lower, device_id_type=MESH)

    @pl.when(above)
    def _():
        pl.semaphore_signal(barrier, inc=1, device_id=upper, device_id_type=MESH)

    load_kap.start()

    @pl.when(swapped)
    def _():
        load_home.start()

    @pl.when(stays)
    def _():
        for c in keep:
            c.start()
        keep_rows.start()

    sub = lax.broadcasted_iota(jnp.int32, (CHUNK, WIDTH), 0)
    lane = lax.broadcasted_iota(jnp.int32, (CHUNK, WIDTH), 1)
    group = lane // 8
    low = lane % 8 < 4
    across_seam = (lane < 4) | (lane >= WIDTH - 4)

    def empty_levels(start):
        @pl.loop(0, 4)
        def _(l):
            for f in range(FIELDS):
                for i in range(CHUNKS):
                    a[f, start + l, ext_rows(i), :] = jnp.zeros((CHUNK, WIDTH), jnp.float32)
                    b[f, start + l, ext_rows(i), :] = jnp.zeros((CHUNK, WIDTH), jnp.float32)

    @pl.when(at_rad == 0)
    def _():
        empty_levels(0)

    @pl.when(at_rad == rads - 1)
    def _():
        empty_levels(4 + LEVELS)

    def put_edges(held, l, tiles):
        held = list(held)
        for f in range(FIELDS):
            at = 8 * (f % 2) + l
            held[f // 2] = jnp.where(group == at, pltpu.roll(tiles[f], (8 * at + 4) % WIDTH, 1), held[f // 2])
        return held

    def packed(src, level, row):
        held = [jnp.zeros((CHUNK, WIDTH), jnp.float32)] * 3
        for l in range(LEVELS):
            held = put_edges(held, l, [src[f, level + l, pl.ds(row, CHUNK), :] for f in range(FIELDS)])
        return held

    def post_edges(posted, i, held):
        posted[0, i, 0] = jnp.where(low, pltpu.roll(held[1], WIDTH - 4, 1), held[0])
        posted[0, i, 1] = held[2]
        posted[1, i, 0] = jnp.where(low, held[0], pltpu.roll(held[1], 4, 1))
        posted[1, i, 1] = held[2]

    def pole_rows(sec, src, level, row):
        mirror = lax.rem(11 - sub, 8)

        @pl.loop(0, LEVELS)
        def _(l):
            for f in range(FIELDS):
                value = jnp.take_along_axis(src[f, level + l, pl.ds(row, CHUNK), :], mirror, axis=0)
                pole_out[sec, f, l] = (-value if flip[f] < 0 else value)[:4]

    pl.semaphore_wait(
        barrier, 3 + swapped.astype(jnp.int32) + below.astype(jnp.int32) + above.astype(jnp.int32)
    )

    move = [
        remote(state.at[:, :, rows_of(i), :], a.at[:, own, ext_rows(i), :], in_send.at[i], in_recv.at[i], partner)
        for i in range(CHUNKS)
    ]
    move_rows = remote(outer, rows_in, rows_send, rows_recv, partner)
    move_kap = remote(kap_out, kap_in, kap_send, kap_recv, partner)
    poles = [
        remote(pole_out.at[n], pole_in.at[n], pole_send.at[n], pole_recv.at[n], across) for n in range(2)
    ]

    def edges(sec, i):
        return (
            remote(edge_out.at[sec, 0, i], edge_in.at[sec, 1, i], edge_send.at[sec, 0, i], edge_recv.at[sec, 1, i], left),
            remote(edge_out.at[sec, 1, i], edge_in.at[sec, 0, i], edge_send.at[sec, 1, i], edge_recv.at[sec, 0, i], right),
        )

    def halo(sec, i, src, down_level, ext):
        buffer = a if sec == 0 else b
        rows = ext_rows(i) if ext else rows_of(i)
        down = remote(
            src.at[:, pl.ds(down_level, 4), rows, :], buffer.at[:, pl.ds(4 + LEVELS, 4), ext_rows(i), :],
            lev_send.at[sec, 0, i], lev_recv.at[sec, 1, i], lower,
        )
        up = remote(
            src.at[:, pl.ds(down_level + 4, 4), rows, :], buffer.at[:, pl.ds(0, 4), ext_rows(i), :],
            lev_send.at[sec, 1, i], lev_recv.at[sec, 0, i], upper,
        )
        return down, up

    def send_levels(sec, i, src, level, ext):
        down, up = halo(sec, i, src, level, ext)

        @pl.when(below)
        def _():
            down.start()

        @pl.when(above)
        def _():
            up.start()

    def await_levels(sec, i):
        down, up = halo(sec, i, a if sec == 0 else b, 4, True)

        @pl.when(below)
        def _():
            up.wait_recv()

        @pl.when(above)
        def _():
            down.wait_recv()

    def each_edge(sec, i, act):
        to_left, to_right = edges(sec, i)
        if sec == 1:
            act(to_left)
            act(to_right)
        else:

            @pl.when(stays | (side_of_pair == 0))
            def _():
                act(to_left)

            @pl.when(stays | (side_of_pair == 1))
            def _():
                act(to_right)

    home_edges = [
        remote(home_out.at[1 - home_side, i], edge_in.at[0, home_side, i], home_send.at[i],
               edge_recv.at[0, home_side, i], sibling)
        for i in range(CHUNKS)
    ]

    def send_edges(sec, i, src):
        if sec == 0:
            held = packed(src, 4, 8 + CHUNK * i)
        else:
            held = [edge_own[i, n] for n in range(3)]
        post_edges(edge_out.at[sec], i, held)
        each_edge(sec, i, lambda c: c.start())
        if i == 0:
            pole_rows(sec, src, 4, 8)
            poles[sec].start()

    @pl.when(swapped)
    def _():
        for c in move[:2]:
            c.start()

    load_kap.wait()
    kap = jnp.full((LEVELS, WIDTH), kap_s[0], jnp.float32)
    for l in range(1, LEVELS):
        kap = jnp.where(sub == l, kap_s[l], kap)
    kap = kap * (time_step * second_coeffs[1])
    kap_out[...] = kap

    @pl.when(stays)
    def _():
        kap_in[...] = kap

    @pl.when(swapped)
    def _():
        move_kap.start()
        for c in move[2:AHEAD]:
            c.start()

    @pl.when(stays)
    def _():
        for i in range(CHUNKS):
            send_levels(0, i, state, 0, False)

    @pl.when(stays)
    def _():
        for i in range(CHUNKS):
            keep[i].wait()
            send_edges(0, i, a)

    @pl.when(swapped)
    def _():
        load_home.wait()

        @pl.loop(0, CHUNKS)
        def _(i):
            post_edges(home_out, i, packed(home, 0, pl.multiple_of(CHUNK * i, CHUNK)))

        for c in home_edges:
            c.start()

    edge_own[...] = jnp.zeros_like(edge_own)
    tap = lax.broadcasted_iota(jnp.int32, (WIDTH, WIDTH), 0) - lax.broadcasted_iota(jnp.int32, (WIDTH, WIDTH), 1)
    for n, (weights, sign) in enumerate(((first_taps, -1.0), (second_taps, 1.0))):
        matrix = jnp.zeros((WIDTH, WIDTH), jnp.float32)
        for k in range(1, 5):
            matrix = jnp.where(tap == k, weights[k - 1], jnp.where(tap == -k, sign * weights[k - 1], matrix))
        for part in range(3):
            taps[n, pl.ds(WIDTH * part, WIDTH), :] = matrix.astype(jnp.bfloat16)

    spacing = 2.0 * math.pi / (WIDTH * lons)

    first_ratio = [c / first_coeffs[0] for c in first_coeffs]
    second_ratio = [e / second_coeffs[1] for e in second_coeffs[1:]]
    step = time_step * first_coeffs[0]

    def weighed(terms, ratios):
        return terms[0] + ratios[1] * terms[1] + ratios[2] * terms[2] + ratios[3] * terms[3]

    def summed(terms, weights):
        return weights[0] * terms[0] + weights[1] * terms[1] + weights[2] * terms[2] + weights[3] * terms[3]

    def seam(sec, i):
        left = [edge_in[sec, 0, i, n] for n in range(2)]
        right = [edge_in[sec, 1, i, n] for n in range(2)]
        beyond = (
            jnp.where(low, left[0], right[0]),
            jnp.where(low, pltpu.roll(left[0], WIDTH - 4, 1), pltpu.roll(right[0], 4, 1)),
            jnp.where(low, left[1], right[1]),
        )
        found = []
        for n in range(3):
            lack = beyond[n]
            on_right = jnp.where(low, 0.0, lack)
            on_left = jnp.where(low, lack, 0.0)
            ahead = [pltpu.roll(on_right, WIDTH - k, 1) for k in range(1, 5)]
            behind = [pltpu.roll(on_left, k, 1) for k in range(1, 5)]
            d = jnp.where(low, summed(ahead, first_taps), -summed(behind, first_taps))
            if n == 2:
                e = jnp.where(low, summed(ahead, second_taps), summed(behind, second_taps))
                d = jnp.where(lane < 64, d, pltpu.roll(e, 64, 1))
            found.append(d)
        return found

    def along_lon(src, i):
        q = src[:, own, ext_rows(i), :].reshape(FIELDS * LEVELS * CHUNK, WIDTH)
        high = q.astype(jnp.bfloat16)
        rest = q - high.astype(jnp.float32)
        middle = rest.astype(jnp.bfloat16)
        last = (rest - middle.astype(jnp.float32)).astype(jnp.bfloat16)
        parts = jnp.concatenate([high, middle, last], axis=1)
        slope = jnp.dot(parts, taps[0], preferred_element_type=jnp.float32)
        along[:FIELDS] = slope.reshape(FIELDS, LEVELS, CHUNK, WIDTH)
        second = jnp.dot(parts[4 * LEVELS * CHUNK :], taps[1], preferred_element_type=jnp.float32)
        along[FIELDS] = second.reshape(LEVELS, CHUNK, WIDTH)

    def across_rows_and_levels(src, i):
        row = 8 + CHUNK * i
        for f in range(FIELDS):
            column = [src[f, n, ext_rows(i), :] for n in range(LEVELS + 8)]
            for l in range(LEVELS):
                row_d, lev_d, row_s, lev_s = [], [], [], []
                for k in range(1, 5):
                    south = src[f, l + 4, pl.ds(row + k, CHUNK), :]
                    north = src[f, l + 4, pl.ds(row - k, CHUNK), :]
                    over, under = column[l + 4 + k], column[l + 4 - k]
                    row_d.append(south - north)
                    lev_d.append(over - under)
                    if f == 4:
                        row_s.append(south + north)
                        lev_s.append(over + under)
                south_d[f, l] = weighed(row_d, first_ratio)
                up_d[f, l] = weighed(lev_d, first_ratio)
                if f == 4:
                    rest[l] = weighed(row_s, second_ratio) + (radial_ratio * radial_ratio) * weighed(
                        lev_s, second_ratio
                    )

    def tendency(src, i, l, extra, consts):
        stretch, turn, stretch2, centre = consts
        cells = [src[f, l + 4, ext_rows(i), :] for f in range(FIELDS)]
        _, u_lon, u_row, u_lev, temper = cells

        def seam_of(n, at):
            return jnp.where(across_seam, pltpu.roll(extra[n], WIDTH - 4 - 8 * at, 1), 0.0)

        by_lon = [along[f, l] + seam_of(f // 2, 8 * (f % 2) + l) for f in range(FIELDS)]
        by_rows = [south_d[f, l] for f in range(FIELDS)]
        by_level = [up_d[f, l] for f in range(FIELDS)]
        laplace = stretch2 * (along[FIELDS, l] + seam_of(2, 8 + l)) + rest[l] + centre * temper
        to_lon, to_row, to_lev = stretch * u_lon, step * u_row, (radial_ratio * step) * u_lev
        carried = [to_lon * by_lon[f] + to_row * by_rows[f] + to_lev * by_level[f] for f in range(FIELDS)]
        spread = stretch * by_lon[1] + step * (by_rows[2] + radial_ratio * by_level[3]) + turn * u_row
        kap_l = jnp.broadcast_to(kap_in[pl.ds(l, 1), :], (CHUNK, WIDTH))
        return cells, [
            carried[0] + spread,
            carried[1] + stretch * (temper * by_lon[0] + by_lon[4]),
            carried[2] + step * (temper * by_rows[0] + by_rows[4]),
            carried[3] + (radial_ratio * step) * (temper * by_level[0] + by_level[4]),
            carried[4] + (gamma_less_one * temper) * spread - kap_l * laplace,
        ]

    def geometry(i):
        thetas = [(CHUNK * i + r + 0.5) * spacing for r in range(CHUNK)]
        metric = [1.0 / math.sin(t) for t in thetas]
        return (
            by_row([time_step / 840 * m for m in metric], sub),
            by_row([time_step * math.cos(t) * m for t, m in zip(thetas, metric)], sub),
            by_row([m * m / second_taps[0] for m in metric], sub),
            by_row([second_coeffs[0] / second_coeffs[1] * (m * m + 1 + radial_ratio**2) for m in metric], sub),
        )

    def first_section(i):
        consts = geometry(i)
        extra = seam(0, i)
        along_lon(a, i)
        across_rows_and_levels(a, i)

        @pl.loop(0, LEVELS, unroll=UNROLL)
        def _(l):
            cells, rate = tendency(a, i, l, extra, consts)
            new = []
            for f in range(FIELDS):
                first[f, l, rows_of(i), :] = rate[f]
                new.append(cells[f] - rate[f])
                b[f, l + 4, ext_rows(i), :] = new[f]
            held = put_edges([edge_own[i, n] for n in range(3)], l, new)
            for n in range(3):
                edge_own[i, n] = held[n]

    def second_section(i):
        consts = geometry(i)
        extra = seam(1, i)
        along_lon(b, i)
        across_rows_and_levels(b, i)

        @pl.loop(0, LEVELS, unroll=UNROLL)
        def _(l):
            _, rate = tendency(b, i, l, extra, consts)
            for f in range(FIELDS):
                total[f, l, rows_of(i), :] = -0.5 * (first[f, l, rows_of(i), :] + rate[f])

    def take_pole(sec, dst):
        poles[sec].wait_recv()

        @pl.loop(0, LEVELS)
        def _(l):
            for f in range(FIELDS):
                dst[f, l + 4, pl.ds(4, 4), :] = pole_in[sec, f, l]

    give = [
        remote(total.at[:, :, rows_of(i), :], out.at[:, :, rows_of(i), :], out_send.at[i], out_recv.at[i], partner)
        for i in range(CHUNKS)
    ]
    put = [
        pltpu.make_async_copy(total.at[:, :, rows_of(i), :], out.at[:, :, rows_of(i), :], out_send.at[i])
        for i in range(CHUNKS)
    ]

    def finish(i, copies):
        if i == 0:
            take_pole(1, b)
        await_levels(1, i)
        for c in edges(1, i):
            c.wait_recv()
        second_section(i)
        copies[i].start()

    for t in range(CHUNKS + 1 + max(LAG, LAG_STAYS)):
        if t < CHUNKS:

            @pl.when(swapped)
            def _():
                move[t].wait_recv()
                send_levels(0, t, a, 4, True)
                send_edges(0, t, a)

        i = t - 1
        if i == 0:
            take_pole(0, a)

            @pl.when(swapped)
            def _():
                move_kap.wait_recv()

        if i == CHUNKS - 1:

            @pl.when(swapped)
            def _():
                move_rows.wait_recv()

            @pl.when(stays)
            def _():
                keep_rows.wait()

            @pl.loop(0, LEVELS)
            def _(l):
                for f in range(FIELDS):
                    a[f, l + 4, pl.ds(8 + ROWS, 4), :] = rows_in[f, l]
                    b[f, l + 4, pl.ds(8 + ROWS, 4), :] = rows_in[f, l]

        if 0 <= i < CHUNKS:
            await_levels(0, i)
            for c in edges(0, i):
                c.wait_recv()
            first_section(i)
            send_levels(1, i, b, 4, True)
            send_edges(1, i, b)
        if t + AHEAD < CHUNKS:

            @pl.when(swapped)
            def _():
                move[t + AHEAD].start()
                if t + AHEAD == CHUNKS - 1:
                    move_rows.start()
        if 0 <= t - 1 - LAG < CHUNKS:

            @pl.when(swapped)
            def _():
                finish(t - 1 - LAG, give)

        if 0 <= t - 1 - LAG_STAYS < CHUNKS:

            @pl.when(stays)
            def _():
                finish(t - 1 - LAG_STAYS, put)

    for c in poles:
        c.wait_send()
    for i in range(CHUNKS):
        for sec in range(2):
            each_edge(sec, i, lambda c: c.wait_send())
            down, up = halo(sec, i, a if sec == 0 else b, 4, True)

            @pl.when(below)
            def _():
                down.wait_send()

            @pl.when(above)
            def _():
                up.wait_send()

    @pl.when(stays)
    def _():
        for c in put:
            c.wait()

    @pl.when(swapped)
    def _():
        for c in (*move, *home_edges, move_rows, move_kap):
            c.wait_send()
        for c in give:
            c.wait()


def solution(mesh):
    lons, rads = mesh.shape["lon"], mesh.shape["rad"]

    def on_device(state, outer_rows, kappa):
        f32 = jnp.float32
        vmem, dma = pltpu.VMEM, pltpu.SemaphoreType.DMA
        block = (FIELDS, LEVELS, ROWS, WIDTH)
        wide = (FIELDS, LEVELS + 8, ROWS + 16, WIDTH)
        edges = (2, 2, CHUNKS, 2, CHUNK, WIDTH)
        own_edges = (CHUNKS, 3, CHUNK, WIDTH)
        pole = (2, FIELDS, LEVELS, 4, WIDTH)
        return pl.pallas_call(
            functools.partial(kernel, lons, rads),
            out_shape=jax.ShapeDtypeStruct(block, f32),
            in_specs=[
                pl.BlockSpec(memory_space=pltpu.HBM),
                pl.BlockSpec(memory_space=pltpu.HBM),
                pl.BlockSpec(memory_space=pltpu.HBM),
            ],
            out_specs=pl.BlockSpec(memory_space=pl.ANY),
            scratch_shapes=[
                vmem(block, f32), vmem((2, CHUNKS, 2, CHUNK, WIDTH), f32),
                vmem(wide, f32), vmem(wide, f32), vmem(block, f32), vmem(block, f32),
                vmem((FIELDS + 1, LEVELS, CHUNK, WIDTH), f32), vmem((FIELDS, LEVELS, CHUNK, WIDTH), f32),
                vmem((FIELDS, LEVELS, CHUNK, WIDTH), f32), vmem((LEVELS, CHUNK, WIDTH), f32),
                vmem(own_edges, f32), vmem(edges, f32), vmem(edges, f32), vmem(pole, f32), vmem(pole, f32),
                vmem((FIELDS, LEVELS, 4, WIDTH), f32), vmem((LEVELS, WIDTH), f32), vmem((LEVELS, WIDTH), f32),
                vmem((2, 3 * WIDTH, WIDTH), jnp.bfloat16), pltpu.SMEM((LEVELS,), f32),
                dma, dma((CHUNKS,)), dma, dma((CHUNKS,)), dma((CHUNKS,)), dma((2, 2, CHUNKS)), dma((2, 2, CHUNKS)),
                dma((2, 2, CHUNKS)), dma((2, 2, CHUNKS)),
                dma((2,)), dma((2,)), dma, dma, dma, dma, dma((CHUNKS,)), dma((CHUNKS,)),
            ],
            compiler_params=pltpu.CompilerParams(
                collective_id=0, has_side_effects=True, vmem_limit_bytes=48_000_000
            ),
        )(*(pltpu.with_memory_space_constraint(x, pltpu.HBM) for x in (state, outer_rows, kappa)))

    placed = (P(None, "rad", None, "lon"), P(None, "rad", None, "lon"), P("rad"))
    return jax.shard_map(
        on_device, mesh=mesh, in_specs=placed, out_specs=P(None, "rad", None, "lon"), check_vma=False
    )
```

```python
import functools
import math

import jax
import jax.numpy as jnp
from jax import lax
from jax.experimental import pallas as pl
from jax.experimental.pallas import tpu as pltpu
from jax.sharding import PartitionSpec as P

first_coeffs = (0.8, -0.2, 4.0 / 105.0, -1.0 / 280.0)
second_coeffs = (-205.0 / 72.0, 1.6, -0.2, 8.0 / 315.0, -1.0 / 560.0)
time_step = 0.002
gamma_less_one = 0.4
radial_ratio = 3.0
first_taps = (672.0, -168.0, 32.0, -3.0)
second_taps = (8064.0, -1008.0, 128.0, -9.0)

FIELDS, LEVELS, ROWS, WIDTH = 5, 8, 48, 128
CHUNK = 8
CHUNKS = ROWS // CHUNK
LAG, LAG_STAYS = 3, 5
AHEAD = 4
UNROLL = 4
MESH = pl.DeviceIdType.MESH
flip = (1.0, -1.0, -1.0, 1.0, 1.0)


def placed_at(lon, rad, lons):
    odd = ((lon // 2) % (lons // 4) + lon // (lons // 2)) % 2
    return (lon // 2) * 2 + (rad + odd) % 2, (rad // 2) * 2 + (lon + odd) % 2


def by_row(values, sub):
    tile = jnp.full((CHUNK, WIDTH), values[0], jnp.float32)
    for r in range(1, CHUNK):
        tile = jnp.where(sub == r, jnp.float32(values[r]), tile)
    return tile


def kernel(
    lons, rads, state, outer, kappa, out,
    home, home_out, a, b, first, total, along, along2, south_d, south2, up_d, rest, rest2, edge_own, edge_out, edge_in, pole_out, pole_in, rows_in, kap_out, kap_in, taps, kap_s,
    home_sem, home_send, kap_sem, in_recv, in_send, lev_recv, lev_send, edge_recv, edge_send,
    pole_recv, pole_send, rows_recv, rows_send, kap_recv, kap_send, out_recv, out_send,
):
    lon, rad = lax.axis_index("lon"), lax.axis_index("rad")
    at_lon, at_rad = placed_at(lon, rad, lons)
    swapped = at_lon != lon
    stays = at_lon == lon
    below, above = at_rad > 0, at_rad < rads - 1
    half = lons // 2
    home_side, side_of_pair = lon % 2, at_lon % 2
    sibling = (lon + 1 - 2 * home_side, rad)

    def around(g, by):
        return lax.rem(g + by + lons, lons)

    partner = (at_lon, at_rad)
    right = placed_at(around(at_lon, 1), at_rad, lons)
    left = placed_at(around(at_lon, -1), at_rad, lons)
    across = placed_at(around(at_lon, half), at_rad, lons)
    lower = placed_at(at_lon, jnp.maximum(at_rad - 1, 0), lons)
    upper = placed_at(at_lon, jnp.minimum(at_rad + 1, rads - 1), lons)
    def remote(src, dst, send, recv, to):
        return pltpu.make_async_remote_copy(
            src_ref=src, dst_ref=dst, send_sem=send, recv_sem=recv, device_id=to, device_id_type=MESH
        )

    def rows_of(i):
        return pl.ds(CHUNK * i, CHUNK)

    def ext_rows(i):
        return pl.ds(8 + CHUNK * i, CHUNK)

    own = pl.ds(4, LEVELS)

    load_home = pltpu.make_async_copy(state, home, home_sem)
    load_kap = pltpu.make_async_copy(kappa, kap_s, kap_sem)
    keep = [
        pltpu.make_async_copy(state.at[:, :, rows_of(i), :], a.at[:, own, ext_rows(i), :], in_recv.at[i])
        for i in range(CHUNKS)
    ]
    keep_rows = pltpu.make_async_copy(outer, rows_in, rows_recv)

    barrier = pltpu.get_barrier_semaphore()
    for peer in (right, left, across):
        pl.semaphore_signal(barrier, inc=1, device_id=peer, device_id_type=MESH)

    @pl.when(swapped)
    def _():
        pl.semaphore_signal(barrier, inc=1, device_id=partner, device_id_type=MESH)

    @pl.when(below)
    def _():
        pl.semaphore_signal(barrier, inc=1, device_id=lower, device_id_type=MESH)

    @pl.when(above)
    def _():
        pl.semaphore_signal(barrier, inc=1, device_id=upper, device_id_type=MESH)

    load_kap.start()

    @pl.when(swapped)
    def _():
        load_home.start()

    @pl.when(stays)
    def _():
        for c in keep:
            c.start()
        keep_rows.start()

    sub = lax.broadcasted_iota(jnp.int32, (CHUNK, WIDTH), 0)
    lane = lax.broadcasted_iota(jnp.int32, (CHUNK, WIDTH), 1)
    group = lane // 8
    low = lane % 8 < 4
    across_seam = (lane < 4) | (lane >= WIDTH - 4)

    def empty_levels(start):
        @pl.loop(0, 4)
        def _(l):
            for f in range(FIELDS):
                for i in range(CHUNKS):
                    a[f, start + l, ext_rows(i), :] = jnp.zeros((CHUNK, WIDTH), jnp.float32)
                    b[f, start + l, ext_rows(i), :] = jnp.zeros((CHUNK, WIDTH), jnp.float32)

    @pl.when(at_rad == 0)
    def _():
        empty_levels(0)

    @pl.when(at_rad == rads - 1)
    def _():
        empty_levels(4 + LEVELS)

    def put_edges(held, l, tiles):
        held = list(held)
        for f in range(FIELDS):
            at = 8 * (f % 2) + l
            held[f // 2] = jnp.where(group == at, pltpu.roll(tiles[f], (8 * at + 4) % WIDTH, 1), held[f // 2])
        return held

    def packed(src, level, row):
        held = [jnp.zeros((CHUNK, WIDTH), jnp.float32)] * 3
        for l in range(LEVELS):
            held = put_edges(held, l, [src[f, level + l, pl.ds(row, CHUNK), :] for f in range(FIELDS)])
        return held

    def post_edges(posted, i, held):
        posted[0, i, 0] = jnp.where(low, pltpu.roll(held[1], WIDTH - 4, 1), held[0])
        posted[0, i, 1] = held[2]
        posted[1, i, 0] = jnp.where(low, held[0], pltpu.roll(held[1], 4, 1))
        posted[1, i, 1] = held[2]

    def pole_rows(sec, src, level, row):
        mirror = lax.rem(11 - sub, 8)

        @pl.loop(0, LEVELS)
        def _(l):
            for f in range(FIELDS):
                value = jnp.take_along_axis(src[f, level + l, pl.ds(row, CHUNK), :], mirror, axis=0)
                pole_out[sec, f, l] = (-value if flip[f] < 0 else value)[:4]

    pl.semaphore_wait(
        barrier, 3 + swapped.astype(jnp.int32) + below.astype(jnp.int32) + above.astype(jnp.int32)
    )

    move = [
        remote(state.at[:, :, rows_of(i), :], a.at[:, own, ext_rows(i), :], in_send.at[i], in_recv.at[i], partner)
        for i in range(CHUNKS)
    ]
    move_rows = remote(outer, rows_in, rows_send, rows_recv, partner)
    move_kap = remote(kap_out, kap_in, kap_send, kap_recv, partner)
    poles = [
        remote(pole_out.at[n], pole_in.at[n], pole_send.at[n], pole_recv.at[n], across) for n in range(2)
    ]

    def edges(sec, i):
        return (
            remote(edge_out.at[sec, 0, i], edge_in.at[sec, 1, i], edge_send.at[sec, 0, i], edge_recv.at[sec, 1, i], left),
            remote(edge_out.at[sec, 1, i], edge_in.at[sec, 0, i], edge_send.at[sec, 1, i], edge_recv.at[sec, 0, i], right),
        )

    def halo(sec, i, src, down_level, ext):
        buffer = a if sec == 0 else b
        rows = ext_rows(i) if ext else rows_of(i)
        down = remote(
            src.at[:, pl.ds(down_level, 4), rows, :], buffer.at[:, pl.ds(4 + LEVELS, 4), ext_rows(i), :],
            lev_send.at[sec, 0, i], lev_recv.at[sec, 1, i], lower,
        )
        up = remote(
            src.at[:, pl.ds(down_level + 4, 4), rows, :], buffer.at[:, pl.ds(0, 4), ext_rows(i), :],
            lev_send.at[sec, 1, i], lev_recv.at[sec, 0, i], upper,
        )
        return down, up

    def send_levels(sec, i, src, level, ext):
        down, up = halo(sec, i, src, level, ext)

        @pl.when(below)
        def _():
            down.start()

        @pl.when(above)
        def _():
            up.start()

    def await_levels(sec, i):
        down, up = halo(sec, i, a if sec == 0 else b, 4, True)

        @pl.when(below)
        def _():
            up.wait_recv()

        @pl.when(above)
        def _():
            down.wait_recv()

    def each_edge(sec, i, act):
        to_left, to_right = edges(sec, i)
        if sec == 1:
            act(to_left)
            act(to_right)
        else:

            @pl.when(stays | (side_of_pair == 0))
            def _():
                act(to_left)

            @pl.when(stays | (side_of_pair == 1))
            def _():
                act(to_right)

    home_edges = [
        remote(home_out.at[1 - home_side, i], edge_in.at[0, home_side, i], home_send.at[i],
               edge_recv.at[0, home_side, i], sibling)
        for i in range(CHUNKS)
    ]

    def send_edges(sec, i, src):
        if sec == 0:
            held = packed(src, 4, 8 + CHUNK * i)
        else:
            held = [edge_own[i, n] for n in range(3)]
        post_edges(edge_out.at[sec], i, held)
        each_edge(sec, i, lambda c: c.start())
        if i == 0:
            pole_rows(sec, src, 4, 8)
            poles[sec].start()

    @pl.when(swapped)
    def _():
        for c in move[:2]:
            c.start()

    load_kap.wait()
    kap = jnp.full((LEVELS, WIDTH), kap_s[0], jnp.float32)
    for l in range(1, LEVELS):
        kap = jnp.where(sub == l, kap_s[l], kap)
    kap = kap * (time_step * second_coeffs[1])
    kap_out[...] = kap

    @pl.when(stays)
    def _():
        kap_in[...] = kap

    @pl.when(swapped)
    def _():
        move_kap.start()
        for c in move[2:AHEAD]:
            c.start()

    @pl.when(stays)
    def _():
        for i in range(CHUNKS):
            send_levels(0, i, state, 0, False)

    @pl.when(stays)
    def _():
        for i in range(CHUNKS):
            keep[i].wait()
            send_edges(0, i, a)

    @pl.when(swapped)
    def _():
        load_home.wait()

        @pl.loop(0, CHUNKS)
        def _(i):
            post_edges(home_out, i, packed(home, 0, pl.multiple_of(CHUNK * i, CHUNK)))

        for c in home_edges:
            c.start()

    edge_own[...] = jnp.zeros_like(edge_own)
    tap = lax.broadcasted_iota(jnp.int32, (WIDTH, WIDTH), 0) - lax.broadcasted_iota(jnp.int32, (WIDTH, WIDTH), 1)
    for n, (weights, sign) in enumerate(((first_taps, -1.0), (second_taps, 1.0))):
        matrix = jnp.zeros((WIDTH, WIDTH), jnp.float32)
        for k in range(1, 5):
            matrix = jnp.where(tap == k, weights[k - 1], jnp.where(tap == -k, sign * weights[k - 1], matrix))
        for part in range(3):
            taps[n, pl.ds(WIDTH * part, WIDTH), :] = matrix.astype(jnp.bfloat16)

    spacing = 2.0 * math.pi / (WIDTH * lons)

    first_ratio = [c / first_coeffs[0] for c in first_coeffs]
    second_ratio = [e / second_coeffs[1] for e in second_coeffs[1:]]
    step = time_step * first_coeffs[0]

    def weighed(terms, ratios):
        return terms[0] + ratios[1] * terms[1] + ratios[2] * terms[2] + ratios[3] * terms[3]

    def summed(terms, weights):
        return weights[0] * terms[0] + weights[1] * terms[1] + weights[2] * terms[2] + weights[3] * terms[3]

    def seam(sec, i):
        left = [edge_in[sec, 0, i, n] for n in range(2)]
        right = [edge_in[sec, 1, i, n] for n in range(2)]
        beyond = (
            jnp.where(low, left[0], right[0]),
            jnp.where(low, pltpu.roll(left[0], WIDTH - 4, 1), pltpu.roll(right[0], 4, 1)),
            jnp.where(low, left[1], right[1]),
        )
        found = []
        for n in range(3):
            lack = beyond[n]
            on_right = jnp.where(low, 0.0, lack)
            on_left = jnp.where(low, lack, 0.0)
            ahead = [pltpu.roll(on_right, WIDTH - k, 1) for k in range(1, 5)]
            behind = [pltpu.roll(on_left, k, 1) for k in range(1, 5)]
            d = jnp.where(low, summed(ahead, first_taps), -summed(behind, first_taps))
            if n == 2:
                e = jnp.where(low, summed(ahead, second_taps), summed(behind, second_taps))
                d = jnp.where(lane < 64, d, pltpu.roll(e, 64, 1))
            found.append(d)
        return found

    def along_lon(src, i, to):
        q = src[:, own, ext_rows(i), :].reshape(FIELDS * LEVELS * CHUNK, WIDTH)
        high = q.astype(jnp.bfloat16)
        rest = q - high.astype(jnp.float32)
        middle = rest.astype(jnp.bfloat16)
        last = (rest - middle.astype(jnp.float32)).astype(jnp.bfloat16)
        parts = jnp.concatenate([high, middle, last], axis=1)
        slope = jnp.dot(parts, taps[0], preferred_element_type=jnp.float32)
        to[:FIELDS] = slope.reshape(FIELDS, LEVELS, CHUNK, WIDTH)
        second = jnp.dot(parts[4 * LEVELS * CHUNK :], taps[1], preferred_element_type=jnp.float32)
        to[FIELDS] = second.reshape(LEVELS, CHUNK, WIDTH)

    def row_slopes(src, i, to, second):
        row = 8 + CHUNK * i
        for f in range(FIELDS):
            for l in range(LEVELS):
                south = [src[f, l + 4, pl.ds(row + k, CHUNK), :] for k in range(1, 5)]
                north = [src[f, l + 4, pl.ds(row - k, CHUNK), :] for k in range(1, 5)]
                to[f, l] = weighed([x - y for x, y in zip(south, north)], first_ratio)
                if f == 4:
                    second[l] = weighed([x + y for x, y in zip(south, north)], second_ratio)

    def level_slopes(src, i, second):
        for f in range(FIELDS):
            column = [src[f, n, ext_rows(i), :] for n in range(LEVELS + 8)]
            for l in range(LEVELS):
                over, under = column[l + 5 : l + 9], column[l : l + 4][::-1]
                up_d[f, l] = weighed([x - y for x, y in zip(over, under)], first_ratio)
                if f == 4:
                    lev_s = weighed([x + y for x, y in zip(over, under)], second_ratio)
                    rest[l] = second[l] + (radial_ratio * radial_ratio) * lev_s

    def tendency(src, i, l, extra, consts, along, south_d):
        stretch, turn, stretch2, centre = consts
        cells = [src[f, l + 4, ext_rows(i), :] for f in range(FIELDS)]
        _, u_lon, u_row, u_lev, temper = cells

        def seam_of(n, at):
            return jnp.where(across_seam, pltpu.roll(extra[n], WIDTH - 4 - 8 * at, 1), 0.0)

        by_lon = [along[f, l] + seam_of(f // 2, 8 * (f % 2) + l) for f in range(FIELDS)]
        by_rows = [south_d[f, l] for f in range(FIELDS)]
        by_level = [up_d[f, l] for f in range(FIELDS)]
        laplace = stretch2 * (along[FIELDS, l] + seam_of(2, 8 + l)) + rest[l] + centre * temper
        to_lon, to_row, to_lev = stretch * u_lon, step * u_row, (radial_ratio * step) * u_lev
        carried = [to_lon * by_lon[f] + to_row * by_rows[f] + to_lev * by_level[f] for f in range(FIELDS)]
        spread = stretch * by_lon[1] + step * (by_rows[2] + radial_ratio * by_level[3]) + turn * u_row
        kap_l = jnp.broadcast_to(kap_in[pl.ds(l, 1), :], (CHUNK, WIDTH))
        return cells, [
            carried[0] + spread,
            carried[1] + stretch * (temper * by_lon[0] + by_lon[4]),
            carried[2] + step * (temper * by_rows[0] + by_rows[4]),
            carried[3] + (radial_ratio * step) * (temper * by_level[0] + by_level[4]),
            carried[4] + (gamma_less_one * temper) * spread - kap_l * laplace,
        ]

    def geometry(i):
        thetas = [(CHUNK * i + r + 0.5) * spacing for r in range(CHUNK)]
        metric = [1.0 / math.sin(t) for t in thetas]
        return (
            by_row([time_step / 840 * m for m in metric], sub),
            by_row([time_step * math.cos(t) * m for t, m in zip(thetas, metric)], sub),
            by_row([m * m / second_taps[0] for m in metric], sub),
            by_row([second_coeffs[0] / second_coeffs[1] * (m * m + 1 + radial_ratio**2) for m in metric], sub),
        )

    def first_section(i):
        consts = geometry(i)
        extra = seam(0, i)
        along_lon(a, i, along)
        row_slopes(a, i, south_d, rest)
        level_slopes(a, i, rest)

        @pl.loop(0, LEVELS, unroll=UNROLL)
        def _(l):
            cells, rate = tendency(a, i, l, extra, consts, along, south_d)
            new = []
            for f in range(FIELDS):
                first[f, l, rows_of(i), :] = rate[f]
                new.append(cells[f] - rate[f])
                b[f, l + 4, ext_rows(i), :] = new[f]
            held = put_edges([edge_own[i, n] for n in range(3)], l, new)
            for n in range(3):
                edge_own[i, n] = held[n]

    def second_section(i):
        consts = geometry(i)
        extra = seam(1, i)
        level_slopes(b, i, rest2.at[i])

        @pl.loop(0, LEVELS, unroll=UNROLL)
        def _(l):
            _, rate = tendency(b, i, l, extra, consts, along2.at[i], south2.at[i])
            for f in range(FIELDS):
                total[f, l, rows_of(i), :] = -0.5 * (first[f, l, rows_of(i), :] + rate[f])

    def take_pole(sec, dst):
        poles[sec].wait_recv()

        @pl.loop(0, LEVELS)
        def _(l):
            for f in range(FIELDS):
                dst[f, l + 4, pl.ds(4, 4), :] = pole_in[sec, f, l]

    give = [
        remote(total.at[:, :, rows_of(i), :], out.at[:, :, rows_of(i), :], out_send.at[i], out_recv.at[i], partner)
        for i in range(CHUNKS)
    ]
    put = [
        pltpu.make_async_copy(total.at[:, :, rows_of(i), :], out.at[:, :, rows_of(i), :], out_send.at[i])
        for i in range(CHUNKS)
    ]

    def finish(i, copies):
        if i == 0:
            take_pole(1, b)
            row_slopes(b, 0, south2.at[0], rest2.at[0])
        await_levels(1, i)
        for c in edges(1, i):
            c.wait_recv()
        second_section(i)
        copies[i].start()

    for t in range(CHUNKS + 1 + max(LAG, LAG_STAYS)):
        if t < CHUNKS:

            @pl.when(swapped)
            def _():
                move[t].wait_recv()
                send_levels(0, t, a, 4, True)
                send_edges(0, t, a)

        i = t - 1
        if i == 0:
            take_pole(0, a)

            @pl.when(swapped)
            def _():
                move_kap.wait_recv()

        if i == CHUNKS - 1:

            @pl.when(swapped)
            def _():
                move_rows.wait_recv()

            @pl.when(stays)
            def _():
                keep_rows.wait()

            @pl.loop(0, LEVELS)
            def _(l):
                for f in range(FIELDS):
                    a[f, l + 4, pl.ds(8 + ROWS, 4), :] = rows_in[f, l]
                    b[f, l + 4, pl.ds(8 + ROWS, 4), :] = rows_in[f, l]

        if 0 <= i < CHUNKS:
            await_levels(0, i)
            for c in edges(0, i):
                c.wait_recv()
            first_section(i)
            send_levels(1, i, b, 4, True)
            send_edges(1, i, b)
        if t + AHEAD < CHUNKS:

            @pl.when(swapped)
            def _():
                move[t + AHEAD].start()
                if t + AHEAD == CHUNKS - 1:
                    move_rows.start()
        if 0 <= t - 1 - LAG < CHUNKS:

            @pl.when(swapped)
            def _():
                finish(t - 1 - LAG, give)

        if 0 <= t - 1 - LAG_STAYS < CHUNKS:

            @pl.when(stays)
            def _():
                finish(t - 1 - LAG_STAYS, put)

        if 0 <= i < CHUNKS:
            along_lon(b, i, along2.at[i])
            for n in range(i - 1, i if i < CHUNKS - 1 else i + 1):
                if n > 0:
                    row_slopes(b, n, south2.at[n], rest2.at[n])

    for c in poles:
        c.wait_send()
    for i in range(CHUNKS):
        for sec in range(2):
            each_edge(sec, i, lambda c: c.wait_send())
            down, up = halo(sec, i, a if sec == 0 else b, 4, True)

            @pl.when(below)
            def _():
                down.wait_send()

            @pl.when(above)
            def _():
                up.wait_send()

    @pl.when(stays)
    def _():
        for c in put:
            c.wait()

    @pl.when(swapped)
    def _():
        for c in (*move, *home_edges, move_rows, move_kap):
            c.wait_send()
        for c in give:
            c.wait()


def solution(mesh):
    lons, rads = mesh.shape["lon"], mesh.shape["rad"]

    def on_device(state, outer_rows, kappa):
        f32 = jnp.float32
        vmem, dma = pltpu.VMEM, pltpu.SemaphoreType.DMA
        block = (FIELDS, LEVELS, ROWS, WIDTH)
        wide = (FIELDS, LEVELS + 8, ROWS + 16, WIDTH)
        edges = (2, 2, CHUNKS, 2, CHUNK, WIDTH)
        own_edges = (CHUNKS, 3, CHUNK, WIDTH)
        tiles = (LEVELS, CHUNK, WIDTH)
        pole = (2, FIELDS, LEVELS, 4, WIDTH)
        return pl.pallas_call(
            functools.partial(kernel, lons, rads),
            out_shape=jax.ShapeDtypeStruct(block, f32),
            in_specs=[
                pl.BlockSpec(memory_space=pltpu.HBM),
                pl.BlockSpec(memory_space=pltpu.HBM),
                pl.BlockSpec(memory_space=pltpu.HBM),
            ],
            out_specs=pl.BlockSpec(memory_space=pl.ANY),
            scratch_shapes=[
                vmem(block, f32), vmem((2, CHUNKS, 2, CHUNK, WIDTH), f32),
                vmem(wide, f32), vmem(wide, f32), vmem(block, f32), vmem(block, f32),
                vmem((FIELDS + 1, *tiles), f32), vmem((CHUNKS, FIELDS + 1, *tiles), f32),
                vmem((FIELDS, *tiles), f32), vmem((CHUNKS, FIELDS, *tiles), f32),
                vmem((FIELDS, *tiles), f32), vmem(tiles, f32), vmem((CHUNKS, *tiles), f32),
                vmem(own_edges, f32), vmem(edges, f32), vmem(edges, f32), vmem(pole, f32), vmem(pole, f32),
                vmem((FIELDS, LEVELS, 4, WIDTH), f32), vmem((LEVELS, WIDTH), f32), vmem((LEVELS, WIDTH), f32),
                vmem((2, 3 * WIDTH, WIDTH), jnp.bfloat16), pltpu.SMEM((LEVELS,), f32),
                dma, dma((CHUNKS,)), dma, dma((CHUNKS,)), dma((CHUNKS,)), dma((2, 2, CHUNKS)), dma((2, 2, CHUNKS)),
                dma((2, 2, CHUNKS)), dma((2, 2, CHUNKS)),
                dma((2,)), dma((2,)), dma, dma, dma, dma, dma((CHUNKS,)), dma((CHUNKS,)),
            ],
            compiler_params=pltpu.CompilerParams(
                collective_id=0, has_side_effects=True, vmem_limit_bytes=48_000_000
            ),
        )(*(pltpu.with_memory_space_constraint(x, pltpu.HBM) for x in (state, outer_rows, kappa)))

    placed = (P(None, "rad", None, "lon"), P(None, "rad", None, "lon"), P("rad"))
    return jax.shard_map(
        on_device, mesh=mesh, in_specs=placed, out_specs=P(None, "rad", None, "lon"), check_vma=False
    )
```

```python
import functools
import math

import jax
import jax.numpy as jnp
from jax import lax
from jax.experimental import pallas as pl
from jax.experimental.pallas import tpu as pltpu
from jax.sharding import PartitionSpec as P

first_coeffs = (0.8, -0.2, 4.0 / 105.0, -1.0 / 280.0)
second_coeffs = (-205.0 / 72.0, 1.6, -0.2, 8.0 / 315.0, -1.0 / 560.0)
time_step = 0.002
gamma_less_one = 0.4
radial_ratio = 3.0
first_taps = (672.0, -168.0, 32.0, -3.0)
second_taps = (8064.0, -1008.0, 128.0, -9.0)

FIELDS, LEVELS, ROWS, WIDTH = 5, 8, 48, 128
CHUNK = 8
CHUNKS = ROWS // CHUNK
LAG, LAG_STAYS = 3, 5
AHEAD = 4
UNROLL = 4
MESH = pl.DeviceIdType.MESH
flip = (1.0, -1.0, -1.0, 1.0, 1.0)


def placed_at(lon, rad, lons):
    odd = ((lon // 2) % (lons // 4) + lon // (lons // 2)) % 2
    return (lon // 2) * 2 + (rad + odd) % 2, (rad // 2) * 2 + (lon + odd) % 2


def by_row(values, sub):
    tile = jnp.full((CHUNK, WIDTH), values[0], jnp.float32)
    for r in range(1, CHUNK):
        tile = jnp.where(sub == r, jnp.float32(values[r]), tile)
    return tile


def kernel(
    lons, rads, state, outer, kappa, out,
    home, home_out, a, b, first, total, along, along2, south_d, south2, up_d, rest, rest2, edge_own, edge_out, edge_in, pole_out, pole_in, rows_in, kap_out, kap_in, taps, kap_s,
    home_sem, home_send, kap_sem, in_recv, in_send, lev_recv, lev_send, edge_recv, edge_send,
    pole_recv, pole_send, rows_recv, rows_send, kap_recv, kap_send, out_recv, out_send,
):
    lon, rad = lax.axis_index("lon"), lax.axis_index("rad")
    at_lon, at_rad = placed_at(lon, rad, lons)
    swapped = at_lon != lon
    stays = at_lon == lon
    below, above = at_rad > 0, at_rad < rads - 1
    half = lons // 2
    home_side, side_of_pair = lon % 2, at_lon % 2
    sibling = (lon + 1 - 2 * home_side, rad)

    def around(g, by):
        return lax.rem(g + by + lons, lons)

    partner = (at_lon, at_rad)
    right = placed_at(around(at_lon, 1), at_rad, lons)
    left = placed_at(around(at_lon, -1), at_rad, lons)
    across = placed_at(around(at_lon, half), at_rad, lons)
    lower = placed_at(at_lon, jnp.maximum(at_rad - 1, 0), lons)
    upper = placed_at(at_lon, jnp.minimum(at_rad + 1, rads - 1), lons)
    def remote(src, dst, send, recv, to):
        return pltpu.make_async_remote_copy(
            src_ref=src, dst_ref=dst, send_sem=send, recv_sem=recv, device_id=to, device_id_type=MESH
        )

    def rows_of(i):
        return pl.ds(CHUNK * i, CHUNK)

    def ext_rows(i):
        return pl.ds(8 + CHUNK * i, CHUNK)

    own = pl.ds(4, LEVELS)

    load_home = pltpu.make_async_copy(state, home, home_sem)
    load_kap = pltpu.make_async_copy(kappa, kap_s, kap_sem)
    keep = [
        pltpu.make_async_copy(state.at[:, :, rows_of(i), :], a.at[:, own, ext_rows(i), :], in_recv.at[i])
        for i in range(CHUNKS)
    ]
    keep_rows = pltpu.make_async_copy(outer, rows_in, rows_recv)

    barrier = pltpu.get_barrier_semaphore()
    for peer in (right, left, across):
        pl.semaphore_signal(barrier, inc=1, device_id=peer, device_id_type=MESH)

    @pl.when(swapped)
    def _():
        pl.semaphore_signal(barrier, inc=1, device_id=partner, device_id_type=MESH)

    @pl.when(below)
    def _():
        pl.semaphore_signal(barrier, inc=1, device_id=lower, device_id_type=MESH)

    @pl.when(above)
    def _():
        pl.semaphore_signal(barrier, inc=1, device_id=upper, device_id_type=MESH)

    load_kap.start()

    @pl.when(swapped)
    def _():
        load_home.start()

    @pl.when(stays)
    def _():
        for c in keep:
            c.start()
        keep_rows.start()

    sub = lax.broadcasted_iota(jnp.int32, (CHUNK, WIDTH), 0)
    lane = lax.broadcasted_iota(jnp.int32, (CHUNK, WIDTH), 1)
    group = lane // 8
    low = lane % 8 < 4
    across_seam = (lane < 4) | (lane >= WIDTH - 4)

    def empty_levels(start):
        @pl.loop(0, 4)
        def _(l):
            for f in range(FIELDS):
                for i in range(CHUNKS):
                    a[f, start + l, ext_rows(i), :] = jnp.zeros((CHUNK, WIDTH), jnp.float32)
                    b[f, start + l, ext_rows(i), :] = jnp.zeros((CHUNK, WIDTH), jnp.float32)

    @pl.when(at_rad == 0)
    def _():
        empty_levels(0)

    @pl.when(at_rad == rads - 1)
    def _():
        empty_levels(4 + LEVELS)

    def put_edges(held, l, tiles):
        held = list(held)
        for f in range(FIELDS):
            at = 8 * (f % 2) + l
            held[f // 2] = jnp.where(group == at, pltpu.roll(tiles[f], (8 * at + 4) % WIDTH, 1), held[f // 2])
        return held

    def packed(src, level, row):
        held = [jnp.zeros((CHUNK, WIDTH), jnp.float32)] * 3
        for l in range(LEVELS):
            held = put_edges(held, l, [src[f, level + l, pl.ds(row, CHUNK), :] for f in range(FIELDS)])
        return held

    def post_edges(posted, i, held):
        posted[0, i, 0] = jnp.where(low, pltpu.roll(held[1], WIDTH - 4, 1), held[0])
        posted[0, i, 1] = held[2]
        posted[1, i, 0] = jnp.where(low, held[0], pltpu.roll(held[1], 4, 1))
        posted[1, i, 1] = held[2]

    def pole_rows(sec, src, level, row):
        mirror = lax.rem(11 - sub, 8)

        @pl.loop(0, LEVELS)
        def _(l):
            for f in range(FIELDS):
                value = jnp.take_along_axis(src[f, level + l, pl.ds(row, CHUNK), :], mirror, axis=0)
                pole_out[sec, f, l] = (-value if flip[f] < 0 else value)[:4]

    pl.semaphore_wait(
        barrier, 3 + swapped.astype(jnp.int32) + below.astype(jnp.int32) + above.astype(jnp.int32)
    )

    move = [
        remote(state.at[:, :, rows_of(i), :], a.at[:, own, ext_rows(i), :], in_send.at[i], in_recv.at[i], partner)
        for i in range(CHUNKS)
    ]
    move_rows = remote(outer, rows_in, rows_send, rows_recv, partner)
    move_kap = remote(kap_out, kap_in, kap_send, kap_recv, partner)
    poles = [
        remote(pole_out.at[n], pole_in.at[n], pole_send.at[n], pole_recv.at[n], across) for n in range(2)
    ]

    def edges(sec, i):
        return (
            remote(edge_out.at[sec, 0, i], edge_in.at[sec, 1, i], edge_send.at[sec, 0, i], edge_recv.at[sec, 1, i], left),
            remote(edge_out.at[sec, 1, i], edge_in.at[sec, 0, i], edge_send.at[sec, 1, i], edge_recv.at[sec, 0, i], right),
        )

    def halo(sec, i, src, down_level, ext):
        buffer = a if sec == 0 else b
        rows = ext_rows(i) if ext else rows_of(i)
        down = remote(
            src.at[:, pl.ds(down_level, 4), rows, :], buffer.at[:, pl.ds(4 + LEVELS, 4), ext_rows(i), :],
            lev_send.at[sec, 0, i], lev_recv.at[sec, 1, i], lower,
        )
        up = remote(
            src.at[:, pl.ds(down_level + 4, 4), rows, :], buffer.at[:, pl.ds(0, 4), ext_rows(i), :],
            lev_send.at[sec, 1, i], lev_recv.at[sec, 0, i], upper,
        )
        return down, up

    def send_levels(sec, i, src, level, ext):
        down, up = halo(sec, i, src, level, ext)

        @pl.when(below)
        def _():
            down.start()

        @pl.when(above)
        def _():
            up.start()

    def await_levels(sec, i):
        down, up = halo(sec, i, a if sec == 0 else b, 4, True)

        @pl.when(below)
        def _():
            up.wait_recv()

        @pl.when(above)
        def _():
            down.wait_recv()

    def each_edge(sec, i, act):
        to_left, to_right = edges(sec, i)
        if sec == 1:
            act(to_left)
            act(to_right)
        else:

            @pl.when(stays | (side_of_pair == 0))
            def _():
                act(to_left)

            @pl.when(stays | (side_of_pair == 1))
            def _():
                act(to_right)

    home_edges = [
        remote(home_out.at[1 - home_side, i], edge_in.at[0, home_side, i], home_send.at[i],
               edge_recv.at[0, home_side, i], sibling)
        for i in range(CHUNKS)
    ]

    def send_edges(sec, i, src):
        if sec == 0:
            held = packed(src, 4, 8 + CHUNK * i)
        else:
            held = [edge_own[i, n] for n in range(3)]
        post_edges(edge_out.at[sec], i, held)
        each_edge(sec, i, lambda c: c.start())
        if i == 0:
            pole_rows(sec, src, 4, 8)
            poles[sec].start()

    @pl.when(swapped)
    def _():
        for c in move[:2]:
            c.start()

    load_kap.wait()
    kap = jnp.full((LEVELS, WIDTH), kap_s[0], jnp.float32)
    for l in range(1, LEVELS):
        kap = jnp.where(sub == l, kap_s[l], kap)
    kap = kap * (time_step * second_coeffs[1])
    kap_out[...] = kap

    @pl.when(stays)
    def _():
        kap_in[...] = kap

    @pl.when(swapped)
    def _():
        move_kap.start()
        for c in move[2:AHEAD]:
            c.start()

    @pl.when(stays)
    def _():
        for i in range(CHUNKS):
            send_levels(0, i, state, 0, False)

    @pl.when(stays)
    def _():
        for i in range(CHUNKS):
            keep[i].wait()
            send_edges(0, i, a)

    @pl.when(swapped)
    def _():
        load_home.wait()

        @pl.loop(0, CHUNKS)
        def _(i):
            post_edges(home_out, i, packed(home, 0, pl.multiple_of(CHUNK * i, CHUNK)))

        for c in home_edges:
            c.start()

    edge_own[...] = jnp.zeros_like(edge_own)
    tap = lax.broadcasted_iota(jnp.int32, (WIDTH, WIDTH), 0) - lax.broadcasted_iota(jnp.int32, (WIDTH, WIDTH), 1)
    for n, (weights, sign) in enumerate(((first_taps, -1.0), (second_taps, 1.0))):
        matrix = jnp.zeros((WIDTH, WIDTH), jnp.float32)
        for k in range(1, 5):
            matrix = jnp.where(tap == k, weights[k - 1], jnp.where(tap == -k, sign * weights[k - 1], matrix))
        for part in range(3):
            taps[n, pl.ds(WIDTH * part, WIDTH), :] = matrix.astype(jnp.bfloat16)

    spacing = 2.0 * math.pi / (WIDTH * lons)

    first_ratio = [c / first_coeffs[0] for c in first_coeffs]
    second_ratio = [e / second_coeffs[1] for e in second_coeffs[1:]]
    step = time_step * first_coeffs[0]

    def weighed(terms, ratios):
        return terms[0] + ratios[1] * terms[1] + ratios[2] * terms[2] + ratios[3] * terms[3]

    def summed(terms, weights):
        return weights[0] * terms[0] + weights[1] * terms[1] + weights[2] * terms[2] + weights[3] * terms[3]

    def seam(sec, i):
        left = [edge_in[sec, 0, i, n] for n in range(2)]
        right = [edge_in[sec, 1, i, n] for n in range(2)]
        beyond = (
            jnp.where(low, left[0], right[0]),
            jnp.where(low, pltpu.roll(left[0], WIDTH - 4, 1), pltpu.roll(right[0], 4, 1)),
            jnp.where(low, left[1], right[1]),
        )
        found = []
        for n in range(3):
            lack = beyond[n]
            on_right = jnp.where(low, 0.0, lack)
            on_left = jnp.where(low, lack, 0.0)
            ahead = [pltpu.roll(on_right, WIDTH - k, 1) for k in range(1, 5)]
            behind = [pltpu.roll(on_left, k, 1) for k in range(1, 5)]
            d = jnp.where(low, summed(ahead, first_taps), -summed(behind, first_taps))
            if n == 2:
                e = jnp.where(low, summed(ahead, second_taps), summed(behind, second_taps))
                d = jnp.where(lane < 64, d, pltpu.roll(e, 64, 1))
            found.append(d)
        return found

    def along_lon(src, i, to):
        q = src[:, own, ext_rows(i), :].reshape(FIELDS * LEVELS * CHUNK, WIDTH)
        high = q.astype(jnp.bfloat16)
        rest = q - high.astype(jnp.float32)
        middle = rest.astype(jnp.bfloat16)
        last = (rest - middle.astype(jnp.float32)).astype(jnp.bfloat16)
        parts = jnp.concatenate([high, middle, last], axis=1)
        slope = jnp.dot(parts, taps[0], preferred_element_type=jnp.float32)
        to[:FIELDS] = slope.reshape(FIELDS, LEVELS, CHUNK, WIDTH)
        second = jnp.dot(parts[4 * LEVELS * CHUNK :], taps[1], preferred_element_type=jnp.float32)
        to[FIELDS] = second.reshape(LEVELS, CHUNK, WIDTH)

    def row_slopes(src, i, to, second):
        row = 8 + CHUNK * i
        for f in range(FIELDS):
            for l in range(LEVELS):
                south = [src[f, l + 4, pl.ds(row + k, CHUNK), :] for k in range(1, 5)]
                north = [src[f, l + 4, pl.ds(row - k, CHUNK), :] for k in range(1, 5)]
                to[f, l] = weighed([x - y for x, y in zip(south, north)], first_ratio)
                if f == 4:
                    second[l] = weighed([x + y for x, y in zip(south, north)], second_ratio)

    def level_slopes(src, i, second):
        for f in range(FIELDS):
            column = [src[f, n, ext_rows(i), :] for n in range(LEVELS + 8)]
            for l in range(LEVELS):
                over, under = column[l + 5 : l + 9], column[l : l + 4][::-1]
                up_d[f, l] = weighed([x - y for x, y in zip(over, under)], first_ratio)
                if f == 4:
                    lev_s = weighed([x + y for x, y in zip(over, under)], second_ratio)
                    rest[l] = second[l] + (radial_ratio * radial_ratio) * lev_s

    def tendency(src, i, l, extra, consts, along, south_d):
        stretch, turn, stretch2, centre = consts
        cells = [src[f, l + 4, ext_rows(i), :] for f in range(FIELDS)]
        _, u_lon, u_row, u_lev, temper = cells

        def seam_of(n, at):
            return jnp.where(across_seam, pltpu.roll(extra[n], WIDTH - 4 - 8 * at, 1), 0.0)

        by_lon = [along[f, l] + seam_of(f // 2, 8 * (f % 2) + l) for f in range(FIELDS)]
        by_rows = [south_d[f, l] for f in range(FIELDS)]
        by_level = [up_d[f, l] for f in range(FIELDS)]
        laplace = stretch2 * (along[FIELDS, l] + seam_of(2, 8 + l)) + rest[l] + centre * temper
        to_lon, to_row, to_lev = stretch * u_lon, step * u_row, (radial_ratio * step) * u_lev
        carried = [to_lon * by_lon[f] + to_row * by_rows[f] + to_lev * by_level[f] for f in range(FIELDS)]
        spread = stretch * by_lon[1] + step * (by_rows[2] + radial_ratio * by_level[3]) + turn * u_row
        kap_l = jnp.broadcast_to(kap_in[pl.ds(l, 1), :], (CHUNK, WIDTH))
        return cells, [
            carried[0] + spread,
            carried[1] + stretch * (temper * by_lon[0] + by_lon[4]),
            carried[2] + step * (temper * by_rows[0] + by_rows[4]),
            carried[3] + (radial_ratio * step) * (temper * by_level[0] + by_level[4]),
            carried[4] + (gamma_less_one * temper) * spread - kap_l * laplace,
        ]

    def geometry(i):
        thetas = [(CHUNK * i + r + 0.5) * spacing for r in range(CHUNK)]
        metric = [1.0 / math.sin(t) for t in thetas]
        return (
            by_row([time_step / 840 * m for m in metric], sub),
            by_row([time_step * math.cos(t) * m for t, m in zip(thetas, metric)], sub),
            by_row([m * m / second_taps[0] for m in metric], sub),
            by_row([second_coeffs[0] / second_coeffs[1] * (m * m + 1 + radial_ratio**2) for m in metric], sub),
        )

    def first_section(i):
        consts = geometry(i)
        extra = seam(0, i)
        along_lon(a, i, along)
        row_slopes(a, i, south_d, rest)
        level_slopes(a, i, rest)

        @pl.loop(0, LEVELS, unroll=UNROLL)
        def _(l):
            cells, rate = tendency(a, i, l, extra, consts, along, south_d)
            new = []
            for f in range(FIELDS):
                first[f, l, rows_of(i), :] = rate[f]
                new.append(cells[f] - rate[f])
                b[f, l + 4, ext_rows(i), :] = new[f]
            held = put_edges([edge_own[i, n] for n in range(3)], l, new)
            for n in range(3):
                edge_own[i, n] = held[n]

    def second_section(i, copies):
        consts = geometry(i)
        extra = seam(1, i)
        level_slopes(b, i, rest2.at[i])

        for part in range(2):

            @pl.loop(4 * part, 4 * part + 4, unroll=UNROLL)
            def _(l):
                _, rate = tendency(b, i, l, extra, consts, along2.at[i], south2.at[i])
                for f in range(FIELDS):
                    total[f, l, rows_of(i), :] = -0.5 * (first[f, l, rows_of(i), :] + rate[f])

            copies[part].start()

    def take_pole(sec, dst):
        poles[sec].wait_recv()

        @pl.loop(0, LEVELS)
        def _(l):
            for f in range(FIELDS):
                dst[f, l + 4, pl.ds(4, 4), :] = pole_in[sec, f, l]

    def part_of(ref, i, part):
        return ref.at[:, pl.ds(4 * part, 4), rows_of(i), :]

    give = [
        [
            remote(part_of(total, i, n), part_of(out, i, n), out_send.at[i, n], out_recv.at[i, n], partner)
            for n in range(2)
        ]
        for i in range(CHUNKS)
    ]
    put = [
        [pltpu.make_async_copy(part_of(total, i, n), part_of(out, i, n), out_send.at[i, n]) for n in range(2)]
        for i in range(CHUNKS)
    ]

    def finish(i, copies):
        if i == 0:
            take_pole(1, b)
            row_slopes(b, 0, south2.at[0], rest2.at[0])
        await_levels(1, i)
        for c in edges(1, i):
            c.wait_recv()
        second_section(i, copies[i])

    for t in range(CHUNKS + 1 + max(LAG, LAG_STAYS)):
        if t < CHUNKS:

            @pl.when(swapped)
            def _():
                move[t].wait_recv()
                send_levels(0, t, a, 4, True)
                send_edges(0, t, a)

        i = t - 1
        if i == 0:
            take_pole(0, a)

            @pl.when(swapped)
            def _():
                move_kap.wait_recv()

        if i == CHUNKS - 1:

            @pl.when(swapped)
            def _():
                move_rows.wait_recv()

            @pl.when(stays)
            def _():
                keep_rows.wait()

            @pl.loop(0, LEVELS)
            def _(l):
                for f in range(FIELDS):
                    a[f, l + 4, pl.ds(8 + ROWS, 4), :] = rows_in[f, l]
                    b[f, l + 4, pl.ds(8 + ROWS, 4), :] = rows_in[f, l]

        if 0 <= i < CHUNKS:
            await_levels(0, i)
            for c in edges(0, i):
                c.wait_recv()
            first_section(i)
            send_levels(1, i, b, 4, True)
            send_edges(1, i, b)
        if t + AHEAD < CHUNKS:

            @pl.when(swapped)
            def _():
                move[t + AHEAD].start()
                if t + AHEAD == CHUNKS - 1:
                    move_rows.start()
        if 0 <= t - 1 - LAG < CHUNKS:

            @pl.when(swapped)
            def _():
                finish(t - 1 - LAG, give)

        if 0 <= t - 1 - LAG_STAYS < CHUNKS:

            @pl.when(stays)
            def _():
                finish(t - 1 - LAG_STAYS, put)

        if 0 <= i < CHUNKS:
            along_lon(b, i, along2.at[i])
            for n in range(i - 1, i if i < CHUNKS - 1 else i + 1):
                if n > 0:
                    row_slopes(b, n, south2.at[n], rest2.at[n])

    for c in poles:
        c.wait_send()
    for i in range(CHUNKS):
        for sec in range(2):
            each_edge(sec, i, lambda c: c.wait_send())
            down, up = halo(sec, i, a if sec == 0 else b, 4, True)

            @pl.when(below)
            def _():
                down.wait_send()

            @pl.when(above)
            def _():
                up.wait_send()

    @pl.when(stays)
    def _():
        for halves in put:
            for c in halves:
                c.wait()

    @pl.when(swapped)
    def _():
        for c in (*move, *home_edges, move_rows, move_kap):
            c.wait_send()
        for halves in give:
            for c in halves:
                c.wait()


def solution(mesh):
    lons, rads = mesh.shape["lon"], mesh.shape["rad"]

    def on_device(state, outer_rows, kappa):
        f32 = jnp.float32
        vmem, dma = pltpu.VMEM, pltpu.SemaphoreType.DMA
        block = (FIELDS, LEVELS, ROWS, WIDTH)
        wide = (FIELDS, LEVELS + 8, ROWS + 16, WIDTH)
        edges = (2, 2, CHUNKS, 2, CHUNK, WIDTH)
        own_edges = (CHUNKS, 3, CHUNK, WIDTH)
        tiles = (LEVELS, CHUNK, WIDTH)
        pole = (2, FIELDS, LEVELS, 4, WIDTH)
        return pl.pallas_call(
            functools.partial(kernel, lons, rads),
            out_shape=jax.ShapeDtypeStruct(block, f32),
            in_specs=[
                pl.BlockSpec(memory_space=pltpu.HBM),
                pl.BlockSpec(memory_space=pltpu.HBM),
                pl.BlockSpec(memory_space=pltpu.HBM),
            ],
            out_specs=pl.BlockSpec(memory_space=pl.ANY),
            scratch_shapes=[
                vmem(block, f32), vmem((2, CHUNKS, 2, CHUNK, WIDTH), f32),
                vmem(wide, f32), vmem(wide, f32), vmem(block, f32), vmem(block, f32),
                vmem((FIELDS + 1, *tiles), f32), vmem((CHUNKS, FIELDS + 1, *tiles), f32),
                vmem((FIELDS, *tiles), f32), vmem((CHUNKS, FIELDS, *tiles), f32),
                vmem((FIELDS, *tiles), f32), vmem(tiles, f32), vmem((CHUNKS, *tiles), f32),
                vmem(own_edges, f32), vmem(edges, f32), vmem(edges, f32), vmem(pole, f32), vmem(pole, f32),
                vmem((FIELDS, LEVELS, 4, WIDTH), f32), vmem((LEVELS, WIDTH), f32), vmem((LEVELS, WIDTH), f32),
                vmem((2, 3 * WIDTH, WIDTH), jnp.bfloat16), pltpu.SMEM((LEVELS,), f32),
                dma, dma((CHUNKS,)), dma, dma((CHUNKS,)), dma((CHUNKS,)), dma((2, 2, CHUNKS)), dma((2, 2, CHUNKS)),
                dma((2, 2, CHUNKS)), dma((2, 2, CHUNKS)),
                dma((2,)), dma((2,)), dma, dma, dma, dma, dma((CHUNKS, 2)), dma((CHUNKS, 2)),
            ],
            compiler_params=pltpu.CompilerParams(
                collective_id=0, has_side_effects=True, vmem_limit_bytes=48_000_000
            ),
        )(*(pltpu.with_memory_space_constraint(x, pltpu.HBM) for x in (state, outer_rows, kappa)))

    placed = (P(None, "rad", None, "lon"), P(None, "rad", None, "lon"), P("rad"))
    return jax.shard_map(
        on_device, mesh=mesh, in_specs=placed, out_specs=P(None, "rad", None, "lon"), check_vma=False
    )
```
